256 devices in a mesh: cls: 8 (over x, core), ori: 32 (over z, y).
Axes of the slice: x: 4, y: 4, z: 8, core: 2. Of those that a mesh axis runs over, the one named last changes fastest.
Arguments:
- images: bfloat16 [2048, 20480], P('ori'), may hold values from -6 to 6
- projections: bfloat16 [8, 4608, 20480], P('cls', 'ori'), may hold values from -0.0390625 to 0.0390625
- log_prior: float32 [8, 4608], P('cls', 'ori'), may hold values from -4 to 300
- significant: int32 [2048, 4], P('ori'), may hold values from 0 to 31, all different within a row; in each aligned block of 64 rows (0 to 63, 64 to 127, ...) at most 12 rows name the same one
- shell_index: int32 [20480], replicated, may hold values from 0 to 99
- noise_inv: float32 [100], replicated, may hold values from 0.5 to 4
Outputs:
- class_sums: bfloat16 [8, 4608, 20480], P('cls', None, 'ori')
- log_evidence: float32 [2048], P('ori')
The draws below stay inside these ranges and needn't reach their ends.
Inputs may be any that keep to these rules, and one draw needn't show every extreme that they name: `significant`: each row names 4 different blocks. Among the rows of one index of ori no block is named more than 12 times, and some block is named exactly 12 times.
All inputs are finite; a program needn't handle non-finite values.
Results may differ from the reference program's by a relative error of at most 0.0076.
Values may be sent and summed in bfloat16 or wider, within the bound.
A program may use at most 128 MiB of HBM per device.

```python
import math
import jax
import jax.numpy as jnp
import numpy as np
from jax import lax

FREQS = 20480
SHELLS = 100
LISTED = 4
ORI_DEV = 144
IMG_DEV = 64
CAPACITY = 12
CLASSES = 8
ORIENTS = 4608
IMAGES = 2048
N_ORI = 32


def draw_log_prior(key, part):
    base_key = jax.random.fold_in(jax.random.fold_in(key, 11), 0)
    baseline = jnp.clip(jax.random.normal(base_key, (CLASSES, ORIENTS), jnp.float32), -4.0, 4.0)
    return baseline


def set_ends(entries, key, low, largest):
    longest = entries.shape.index(max(entries.shape))
    spots = []
    for shift in (0, 1):
        where = [jax.random.randint(jax.random.fold_in(key, axis), (), 0, length) for axis, length in enumerate(entries.shape)]
        where[longest] = (where[longest] + shift) % entries.shape[longest]
        spots.append(tuple(where))
    return entries.at[spots[0]].set(low).at[spots[1]].set(largest)


def steps_of(key, extent, pieces, least, high):
    def one(position, shards_of):
        heights = jax.random.uniform(jax.random.fold_in(jax.random.fold_in(key, 6), position), (shards_of,), jnp.float32, least / len(pieces), high / len(pieces))
        return jnp.repeat(jnp.exp(heights), extent[position] // shards_of).reshape((-1,) + (1,) * (len(extent) - position - 1))

    level = one(*pieces[0])
    for cut in pieces[1:]:
        level = level * one(*cut)
    return level


def shared_out(rng, own, number, rows, count, top, limit, lean):
    order = jax.random.permutation(rng, count)
    crowded, common = portions_of(count, rows * top, limit, lean, True), portions_of(count, rows * top, limit, lean, False)
    places = jnp.arange(count)

    def named(sizes, offset_by):
        used = int((sizes > 0).sum())
        fixed = max(1, used // 4)
        moved = fixed + (places - fixed + offset_by * (used - fixed)) % max(1, count - fixed)
        return jnp.zeros((count,), jnp.int32).at[order[jnp.where(places < fixed, places, moved)]].set(jnp.asarray(sizes, jnp.int32))

    sizes = jnp.where(number % 4 == 0, named(crowded, number // 4), named(common, number - number // 4 - 1))
    mixed = jax.random.permutation(jax.random.fold_in(own, 3), count)
    donor, sink = mixed[0:count // 2 * 2:2], mixed[1:count // 2 * 2:2]
    margin = jnp.minimum(sizes[donor] - 1, limit - sizes[sink]) // 2
    margin = jnp.where((donor == order[0]) | (sink == order[0]) | (sizes[sink] == 0), 0, jnp.maximum(margin, 0))
    moved = jax.random.randint(jax.random.fold_in(own, 4), (count // 2,), 0, 1 << 20) % (margin + 1)
    sizes = sizes.at[donor].add(-moved).at[sink].add(moved)
    items = jnp.searchsorted(jnp.cumsum(sizes), jnp.arange(rows * top), side="right").astype(jnp.int32)
    table = items.reshape(top, rows).T
    table = table[jax.random.permutation(jax.random.fold_in(own, 1), rows)]
    offset_by = jax.random.randint(jax.random.fold_in(own, 2), (rows, 1), 0, top)
    return jnp.take_along_axis(table, (jnp.arange(top)[None, :] + offset_by) % top, axis=1)


def portions_of(number_of, total, most, slope, full):
    portions = [(1 << 20) // math.isqrt(rank ** slope) + 1 for rank in range(1, number_of + 1)]
    largest = most if full else min(most, max(-(-total // number_of), total * portions[0] // sum(portions)))
    least = 1 if total - largest >= number_of - 1 else 0
    counts, spare = [largest] + [least] * (number_of - 1), total - largest - least * (number_of - 1)
    while spare > 0:
        movable = [i for i in range(1, number_of) if counts[i] < largest] or [i for i in range(1, number_of) if counts[i] < most]
        pool, left = sum([portions[i] for i in movable]), spare
        for i in movable:
            addition = min(most - counts[i], max(1, left * portions[i] // pool), spare)
            counts[i] = counts[i] + addition
            spare = spare - addition
    return np.array(counts)


def bell_draw(rng, extent, width, limit, shards=(), kind=jnp.bfloat16):
    drawn = jax.random.normal(rng, extent, jnp.float32) * width
    if len(shards) > 0:
        drawn = steps_of(rng, extent, shards, -0.22, 0.18) * drawn
    return jnp.clip(drawn, min=-limit, max=limit).astype(kind)


def setup_inputs(seed: int = 0) -> dict:
    arg_keys = jax.random.split(jax.random.key(seed), 7)
    images = bell_draw(arg_keys[0], (IMAGES, FREQS), 1.0, 6.0, ((0, 32),))
    projections = bell_draw(arg_keys[1], (CLASSES, ORIENTS, FREQS), FREQS ** -0.5, 0.0390625, ((0, 8), (1, 32)))
    log_prior = draw_log_prior(jax.random.fold_in(arg_keys[6], 71), 0)
    significant_keys = jax.random.split(jax.random.fold_in(arg_keys[3], 1), IMAGES // IMG_DEV)
    significant_turns = jax.random.permutation(jax.random.fold_in(arg_keys[3], 3), IMAGES // IMG_DEV)
    significant = jax.vmap(lambda own, number: shared_out(jax.random.fold_in(arg_keys[3], 2), own, number, IMG_DEV, N_ORI, LISTED, CAPACITY, 2))(significant_keys, significant_turns).reshape((IMAGES, LISTED))
    shell_index = set_ends(jax.random.randint(arg_keys[4], (FREQS,), 0, SHELLS), jax.random.fold_in(arg_keys[4], 1), 0, SHELLS - 1).astype(jnp.int32)
    noise_inv = jnp.clip(jnp.exp(jax.random.uniform(arg_keys[5], (SHELLS,), jnp.float32, math.log(0.5), math.log(4.0))), 0.5, 4.0)
    return {"images": images, "projections": projections, "log_prior": log_prior, "significant": significant, "shell_index": shell_index, "noise_inv": noise_inv}


SENTINEL = -1e30


def shell_weights(noise_inv, shell_index):
    levels = jnp.arange(noise_inv.shape[0], dtype=jnp.int32)
    table = (shell_index[:, None] == levels[None, :]).astype(jnp.float32)
    return jnp.sum(table * noise_inv[None, :].astype(jnp.float32), axis=1)


def reference(images, projections, log_prior, significant, shell_index, noise_inv):
    weight = shell_weights(noise_inv, shell_index)
    weighted = (images.astype(jnp.float32) * weight[None, :]).astype(jnp.bfloat16)
    weighted_wide = weighted.astype(jnp.float32)
    blocks = jnp.arange(N_ORI, dtype=jnp.int32)
    listed_mask = jnp.any(significant[:, :, None] == blocks[None, None, :], axis=1)
    column_mask = jnp.repeat(listed_mask, ORI_DEV, axis=1)

    def class_scores(inputs):
        projection, prior_row = inputs
        wide = projection.astype(jnp.float32)
        half_norm = 0.5 * jnp.sum(wide * wide * weight[None, :], axis=1)
        scores = jnp.dot(weighted_wide, wide.T, preferred_element_type=jnp.float32)
        scores = scores - half_norm[None, :] + prior_row[None, :]
        return jnp.where(column_mask, scores, SENTINEL)

    scores = lax.map(class_scores, (projections, log_prior))
    highest = jnp.max(jnp.max(scores, axis=2), axis=0)
    shifted = jnp.where(column_mask[None], jnp.exp(scores - highest[None, :, None]), 0.0)
    totals = jnp.sum(jnp.sum(shifted, axis=2), axis=0)
    log_evidence = highest + jnp.log(totals)

    def sums_of_class(class_scores_one):
        posterior = jnp.where(column_mask, jnp.exp(class_scores_one - highest[:, None]) / totals[:, None], 0.0)
        posterior = posterior.astype(jnp.bfloat16).astype(jnp.float32)
        return jnp.dot(posterior.T, weighted_wide, preferred_element_type=jnp.float32).astype(jnp.bfloat16)

    class_sums = lax.map(sums_of_class, scores)
    return class_sums, log_evidence
```

```python
import jax
import jax.numpy as jnp
from jax import lax
from jax.sharding import PartitionSpec as P

SENTINEL = -1e30


def shell_weights(noise_inv, shell_index):
    levels = jnp.arange(noise_inv.shape[0], dtype=jnp.int32)
    table = (shell_index[:, None] == levels[None, :]).astype(jnp.float32)
    return jnp.sum(table * noise_inv[None, :], axis=1)


def body(images, projections, log_prior, significant, shell_index, noise_inv):
    owners = lax.axis_size("ori")
    classes = lax.axis_size("cls")
    own = lax.axis_index("ori")
    cls = lax.axis_index("cls")
    rows, width = images.shape
    listed = significant.shape[1]
    cap = max(2, 3 * rows * listed // (2 * owners))
    slots = owners * cap
    total = owners * rows
    part = width // classes
    col = width // owners
    sub = rows // classes
    orients = projections.shape[1]

    weight = shell_weights(noise_inv, shell_index)
    weighted = (images.astype(jnp.float32) * weight[None, :]).astype(jnp.bfloat16)
    mine = lax.dynamic_slice(weighted, (0, cls * part), (rows, part))
    everyone = lax.all_gather(mine, "ori", axis=0, tiled=True)
    split = projections[0].reshape(orients, classes, part).transpose(1, 0, 2)
    proj = lax.all_to_all(split, "cls", split_axis=0, concat_axis=0, tiled=True)
    weight_part = lax.dynamic_slice(weight, (cls * part,), (part,))
    band = lax.dynamic_slice(weighted, (cls * sub, 0), (sub, width))
    band = band.reshape(sub, owners, col).transpose(1, 0, 2)
    band = lax.all_to_all(band, "ori", split_axis=0, concat_axis=0, tiled=True)
    band = lax.all_gather(band, "cls", axis=0)
    band = band.transpose(1, 0, 2, 3).reshape(total, col)

    listing = lax.all_gather(significant, "ori", axis=0, tiled=True)
    blocks = jnp.arange(owners, dtype=jnp.int32)
    named = jnp.any(listing[:, :, None] == blocks[None, None, :], axis=1).reshape(owners, rows, owners)
    named_int = named.astype(jnp.int32)
    ranks = jnp.cumsum(named_int, axis=1) - named_int
    places = jnp.arange(cap, dtype=jnp.int32)
    chosen = named.transpose(0, 2, 1)[:, :, None, :] & (
        ranks.transpose(0, 2, 1)[:, :, None, :] == places[None, None, :, None]
    )
    ids = jnp.arange(total, dtype=jnp.int32).reshape(owners, rows)
    table = jnp.sum(jnp.where(chosen, ids[:, None, None, :] + 1, 0), axis=3) - 1
    table = table.transpose(1, 0, 2).reshape(owners, slots)
    my_table = lax.dynamic_slice(table, (own, 0), (1, slots))[0]
    filled = my_table >= 0
    every_id = jnp.arange(total, dtype=jnp.int32)
    pick = (my_table[:, None] == every_id[None, :]).astype(jnp.bfloat16)
    received = jnp.dot(pick, everyone, preferred_element_type=jnp.float32).astype(jnp.bfloat16)
    wide = proj.astype(jnp.float32)
    half_norm = 0.5 * jnp.sum(jnp.square(wide) * weight_part[None, None, :], axis=2)
    partial = jnp.einsum("krf,sf->krs", proj, received, preferred_element_type=jnp.float32) - half_norm[:, :, None]
    scores = lax.psum_scatter(partial, "cls", scatter_dimension=0, tiled=True)[0]
    scores = scores + log_prior[0][:, None]
    peak = jnp.where(filled, jnp.max(scores, axis=0), SENTINEL)
    raised = jnp.where(filled[None, :], jnp.exp(scores - peak[None, :]), 0.0)
    amount = jnp.sum(raised, axis=0)
    stats = lax.all_gather(jnp.stack([peak, amount]), "cls", axis=0)
    top = jnp.max(stats[:, 0], axis=0)
    summed = jnp.sum(stats[:, 1] * jnp.exp(stats[:, 0] - top[None, :]), axis=0)
    spread = lax.all_gather(jnp.stack([peak, top, summed]), "ori", axis=0)
    shared = lax.all_gather(raised.astype(jnp.bfloat16), "ori", axis=0)

    def by_source(x):
        return x.reshape(owners, owners, cap).transpose(1, 0, 2)

    top_s = by_source(spread[:, 1])[:, :, :, None]
    sum_s = by_source(spread[:, 2])[:, :, :, None]
    best = jnp.max(jnp.where(chosen, top_s, SENTINEL), axis=(1, 2))
    full = jnp.sum(jnp.where(chosen, sum_s * jnp.exp(top_s - best[:, None, None, :]), 0.0), axis=(1, 2))
    slot_best = jnp.sum(jnp.where(chosen, best[:, None, None, :], 0.0), axis=3)
    slot_full = jnp.sum(jnp.where(chosen, full[:, None, None, :], 0.0), axis=3)
    slot_best = slot_best.transpose(1, 0, 2).reshape(owners, slots)
    slot_full = slot_full.transpose(1, 0, 2).reshape(owners, slots)
    usable = table >= 0
    scale = jnp.where(
        usable, jnp.exp(jnp.where(usable, spread[:, 0] - slot_best, 0.0)) / jnp.where(usable, slot_full, 1.0), 0.0
    )
    posterior = (shared.astype(jnp.float32) * scale[:, None, :]).astype(jnp.bfloat16)
    pick_all = (table.reshape(-1)[:, None] == every_id[None, :]).astype(jnp.bfloat16)
    gathered = jnp.dot(pick_all, band, preferred_element_type=jnp.float32).astype(jnp.bfloat16)
    gathered = gathered.reshape(owners, slots, col)
    sums = jnp.einsum("ors,osf->orf", posterior, gathered, preferred_element_type=jnp.float32).astype(jnp.bfloat16)
    evidence = best + jnp.log(full)
    log_evidence = lax.dynamic_slice(evidence, (own, 0), (1, rows))[0]
    return (sums.reshape(1, owners * orients, col), log_evidence)


def solution(mesh):
    in_specs = (P("ori", None), P("cls", "ori", None), P("cls", "ori"), P("ori", None), P(), P())
    out_specs = (P("cls", None, "ori"), P("ori"))
    return jax.shard_map(body, mesh=mesh, in_specs=in_specs, out_specs=out_specs, check_vma=False)
```

```python
import functools

import jax
import jax.numpy as jnp
from jax import lax
from jax.experimental import pallas as pl
from jax.experimental.pallas import tpu as pltpu
from jax.sharding import PartitionSpec as P

MESH = pl.DeviceIdType.MESH
SENTINEL = -1e30
TILE = 128
NY = 4
NZ = 8
NX = 4


def shell_weights(noise_inv, shell_index):
    levels = jnp.arange(noise_inv.shape[0], dtype=jnp.int32)
    table = (shell_index[:, None] == levels[None, :]).astype(jnp.float32)
    return jnp.sum(table * noise_inv[None, :], axis=1)


def mod(value, size):
    return lax.rem(value + size, size)


def ring_gather(buf, view, pos, sizes, devs, send_sem, recv_sem):
    (f, g), (nf, ng) = pos, sizes
    dev_f, dev_g = devs
    started = []
    offsets = [0]
    for r in range(1, nf // 2):
        offsets += [-r, r]
    offsets.append(nf // 2)

    def rows(r, n, d):
        return d if r == n // 2 - 1 else None

    def copy(ident, fi, gi, part, dev):
        ref = view(buf, mod(fi, nf), mod(gi, ng), part)
        return pltpu.make_async_remote_copy(
            src_ref=ref,
            dst_ref=ref,
            send_sem=send_sem.at[ident],
            recv_sem=recv_sem.at[ident],
            device_id=dev,
            device_id_type=MESH,
        )

    def start_f(r, d):
        sign = 1 - 2 * d
        cp = copy(2 * r + d, f - sign * r, g, rows(r, nf, d), dev_f(sign))
        cp.start()
        started.append(cp)

    def wait_f(r, d):
        sign = 1 - 2 * d
        copy(2 * r + d, f - sign * (r + 1), g, rows(r, nf, d), dev_f(sign)).wait_recv()

    def start_g(j, r, d):
        sign = 1 - 2 * d
        ident = nf + (j * (ng // 2) + r) * 2 + d
        cp = copy(ident, f + offsets[j], g - sign * r, rows(r, ng, d), dev_g(sign))
        cp.start()
        started.append(cp)

    def wait_g(j, r, d):
        sign = 1 - 2 * d
        ident = nf + (j * (ng // 2) + r) * 2 + d
        copy(ident, f + offsets[j], g - sign * (r + 1), rows(r, ng, d), dev_g(sign)).wait_recv()

    for d in (0, 1):
        start_f(0, d)
        start_g(0, 0, d)
    for r in range(nf // 2):
        for d in (0, 1):
            wait_f(r, d)
            if r + 1 < nf // 2:
                start_f(r + 1, d)
        for j in (2 * r + 1, 2 * r + 2):
            if j < nf:
                for d in (0, 1):
                    start_g(j, 0, d)
    for r in range(ng // 2):
        for j in range(nf):
            for d in (0, 1):
                wait_g(j, r, d)
                if r + 1 < ng // 2:
                    start_g(j, r + 1, d)
    for cp in started:
        cp.wait_send()


def exchange_kernel(
    mine_ref,
    proj_ref,
    weight_ref,
    prior_ref,
    shared,
    ranks_ref,
    band,
    images,
    proj,
    received,
    part,
    from_pair,
    summed,
    from_far,
    stat,
    own_sem,
    proj_send,
    proj_recv,
    img_send,
    img_recv,
    post_send,
    post_recv,
    pair_send,
    pair_recv,
    far_send,
    far_recv,
    stat_send,
    stat_recv,
    band_send,
    band_recv,
):
    cls = lax.axis_index("cls")
    ori = lax.axis_index("ori")
    x, core = cls // 2, cls % 2
    z, y = ori // NY, ori % NY
    classes = 2 * NX
    img_rows = images.shape[2]
    width = proj.shape[2]
    col = band.shape[3]
    slots = received.shape[0]
    orients = proj.shape[1]
    cap = slots // (NY * NZ)

    def cls_dev(k):
        return (k, ori)

    def y_dev(sign):
        return (cls, z * NY + mod(y + sign, NY))

    def z_dev(sign):
        return (cls, mod(z + sign, NZ) * NY + y)

    barrier = pltpu.get_barrier_semaphore()
    for d in range(1, classes):
        pl.semaphore_signal(barrier, inc=1, device_id=cls_dev(mod(cls + d, classes)), device_id_type=MESH)
    for sign in (1, -1):
        pl.semaphore_signal(barrier, inc=1, device_id=y_dev(sign), device_id_type=MESH)
        pl.semaphore_signal(barrier, inc=1, device_id=z_dev(sign), device_id_type=MESH)
    own_img = pltpu.make_async_copy(mine_ref, images.at[z, y], own_sem.at[0])
    own_img.start()
    own_proj = pltpu.make_async_copy(
        proj_ref.at[:, pl.ds(pl.multiple_of(cls * width, TILE), width)], proj.at[cls], own_sem.at[1]
    )
    own_proj.start()
    pl.semaphore_wait(barrier, classes + 3)

    def proj_copy(d, to, frm):
        return pltpu.make_async_remote_copy(
            src_ref=proj_ref.at[:, pl.ds(pl.multiple_of(to * width, TILE), width)],
            dst_ref=proj.at[frm],
            send_sem=proj_send.at[d],
            recv_sem=proj_recv.at[d],
            device_id=cls_dev(to),
            device_id_type=MESH,
        )

    for d in range(1, classes):
        proj_copy(d, mod(cls + d, classes), cls).start()
    own_img.wait()

    def image_view(swap):
        def view(buf, fi, gi, half):
            zi, yi = (fi, gi) if swap else (gi, fi)
            n = buf.shape[2]
            if half is None:
                return buf.at[zi, yi]
            return buf.at[zi, yi, pl.ds(half * (n // 2), n // 2)]

        return view

    def gather(buf, send_sem, recv_sem):
        @pl.when(core == 0)
        def _():
            ring_gather(buf, image_view(False), (y, z), (NY, NZ), (y_dev, z_dev), send_sem, recv_sem)

        @pl.when(core == 1)
        def _():
            ring_gather(buf, image_view(True), (z, y), (NZ, NY), (z_dev, y_dev), send_sem, recv_sem)

    gather(images, img_send, img_recv)

    owner_x, owner_core = z // 2, z % 2
    role = mod(x - owner_x, NX)
    on_line = core == owner_core
    pieces = band_recv.shape[0]
    depth = NZ // pieces
    band_cols = pl.ds(pl.multiple_of(y * col, TILE), col)

    def band_copy(j, lane, dev, first):
        zs = pl.ds(j * depth, depth)
        return pltpu.make_async_remote_copy(
            src_ref=images.at[zs, :, :, band_cols] if first else band.at[zs],
            dst_ref=band.at[zs],
            send_sem=band_send.at[lane, j],
            recv_sem=band_recv.at[j],
            device_id=dev,
            device_id_type=MESH,
        )

    ahead = (mod(x + 1, NX) * 2 + core, ori)
    behind = (mod(x - 1, NX) * 2 + core, ori)
    pair = (x * 2 + 1 - core, ori)
    is_owner = jnp.logical_and(on_line, role == 0)

    @pl.when(is_owner)
    def _():
        for j in range(pieces):
            band_copy(j, 0, ahead, True).start()
            band_copy(pieces - 1 - j, 1, behind, True).start()
        for j in range(pieces):
            band_copy(j, 2, pair, True).start()
        keep = pltpu.make_async_copy(images.at[:, :, :, band_cols], band, own_sem.at[2])
        keep.start()
        keep.wait()

    def band_relay(j):
        @pl.when(jnp.logical_and(jnp.logical_not(is_owner), role != 3))
        def _():
            band_copy(j, 0, pair, False).wait_recv()

        @pl.when(role == 3)
        def _():
            band_copy(pieces - 1 - j, 0, pair, False).wait_recv()

        @pl.when(jnp.logical_and(on_line, role == 1))
        def _():
            if j < pieces // 2:
                band_copy(j, 0, ahead, False).start()
            band_copy(j, 2, pair, False).start()

        @pl.when(jnp.logical_and(on_line, role == 3))
        def _():
            if j < pieces // 2:
                band_copy(pieces - 1 - j, 1, behind, False).start()
            band_copy(pieces - 1 - j, 2, pair, False).start()

        @pl.when(jnp.logical_and(on_line, role == 2))
        def _():
            band_copy(j, 2, pair, False).start()

    def band_finish():
        @pl.when(is_owner)
        def _():
            for j in range(pieces):
                for lane in range(3):
                    band_copy(j, lane, pair, True).wait_send()

        @pl.when(jnp.logical_and(on_line, role == 1))
        def _():
            for j in range(pieces // 2):
                band_copy(j, 0, pair, False).wait_send()
            for j in range(pieces):
                band_copy(j, 2, pair, False).wait_send()

        @pl.when(jnp.logical_and(on_line, role == 3))
        def _():
            for j in range(pieces // 2):
                band_copy(pieces - 1 - j, 1, pair, False).wait_send()
            for j in range(pieces):
                band_copy(j, 2, pair, False).wait_send()

        @pl.when(jnp.logical_and(on_line, role == 2))
        def _():
            for j in range(pieces):
                band_copy(j, 2, pair, False).wait_send()

    lanes = NY * img_rows
    lane_src = lax.broadcasted_iota(jnp.int32, (NY * cap, lanes), 1) // img_rows
    row_id = lax.broadcasted_iota(jnp.int32, (NY * cap, lanes), 0)
    same = lane_src == row_id // cap
    place = (row_id % cap).astype(jnp.float32)
    o_row = lax.broadcasted_iota(jnp.int32, (NY * NZ, TILE), 0) == ori
    low = lax.broadcasted_iota(jnp.int32, (1, TILE), 1) < img_rows

    def pack(zi, carry):
        lines = []
        for yi in range(NY):
            table = images[zi, yi, 0 : NY * NZ, width : width + TILE]
            ranks_ref[zi, yi] = table
            lines.append(jnp.sum(jnp.where(o_row, table.astype(jnp.float32), 0.0), axis=0, keepdims=True))
        line = jnp.concatenate([jnp.where(low, lines[0], lines[1]), jnp.where(low, lines[2], lines[3])], axis=1)
        pick = jnp.where(jnp.logical_and(same, place == line), 1.0, 0.0).astype(jnp.bfloat16)
        data = images[zi, :, :, 0:width].reshape(lanes, width)
        found = jnp.dot(pick, data, preferred_element_type=jnp.float32)
        received[pl.ds(pl.multiple_of(zi * NY * cap, 16), NY * cap), :] = found.astype(jnp.bfloat16)
        return carry

    lax.fori_loop(0, NZ, pack, 0)

    own_proj.wait()
    for d in range(1, classes):
        proj_copy(d, mod(cls + d, classes), mod(cls - d, classes)).wait_recv()

    def partial(k):
        block = proj[k]
        score = lax.dot_general(block, received[...], (((1,), (1,)), ((), ())), preferred_element_type=jnp.float32)
        norm = jnp.zeros((orients, TILE), jnp.float32)
        for j in range(width // TILE):
            wide = block[:, j * TILE : (j + 1) * TILE].astype(jnp.float32)
            norm = norm + wide * wide * weight_ref[:, j * TILE : (j + 1) * TILE]
        return score - 0.5 * jnp.sum(norm, axis=1, keepdims=True)

    def pair_copy(j):
        return pltpu.make_async_remote_copy(
            src_ref=part.at[j],
            dst_ref=from_pair.at[j],
            send_sem=pair_send.at[j],
            recv_sem=pair_recv.at[j],
            device_id=pair,
            device_id_type=MESH,
        )

    def far_copy(j, dx):
        return pltpu.make_async_remote_copy(
            src_ref=summed.at[j],
            dst_ref=from_far.at[j],
            send_sem=far_send.at[j],
            recv_sem=far_recv.at[j],
            device_id=(mod(x + dx, NX) * 2 + core, ori),
            device_id_type=MESH,
        )

    def to_pair(t, carry):
        j = lax.rem(t + 2, NX)
        part[j] = partial(mod(x + j, NX) * 2 + 1 - core)
        pair_copy(j).start()
        return carry

    lax.fori_loop(0, NX, to_pair, 0)

    def to_far(t, carry):
        j = lax.rem(t + 2, NX)
        value = partial(mod(x + j, NX) * 2 + core)
        pair_copy(j).wait_recv()
        summed[j] = value + from_pair[j]

        @pl.when(j != 0)
        def _():
            far_copy(j, j).start()

        return carry

    lax.fori_loop(0, NX, to_far, 0)
    band_relay(0)
    total = summed[0]
    for j in range(1, NX):
        far_copy(j, j).wait_recv()
        total = total + from_far[j]
    score = total + prior_ref[...]
    peak = jnp.max(score, axis=0, keepdims=True)
    amount = jnp.sum(jnp.exp(score - peak), axis=0, keepdims=True)
    row8 = lax.broadcasted_iota(jnp.int32, (8, slots), 0)
    stat[cls] = jnp.where(row8 == 0, peak, jnp.where(row8 == 1, amount, 0.0))

    def stat_copy(d, frm):
        return pltpu.make_async_remote_copy(
            src_ref=stat.at[frm],
            dst_ref=stat.at[frm],
            send_sem=stat_send.at[d],
            recv_sem=stat_recv.at[d],
            device_id=cls_dev(mod(cls + d, classes)),
            device_id_type=MESH,
        )

    for d in range(1, classes):
        stat_copy(d, cls).start()
    band_relay(1)
    for d in range(1, classes):
        stat_copy(d, mod(cls - d, classes)).wait_recv()
    top = stat[0, 0:1]
    for k in range(1, classes):
        top = jnp.maximum(top, stat[k, 0:1])
    full = jnp.zeros_like(top)
    for k in range(classes):
        full = full + stat[k, 1:2] * jnp.exp(stat[k, 0:1] - top)
    shared[z, y, 0:orients, :] = jnp.exp(score - top).astype(jnp.bfloat16)
    row16 = lax.broadcasted_iota(jnp.int32, (16, slots), 0)
    tail = jnp.zeros((16, slots), jnp.float32)
    at = 0
    for value in (top, full):
        for _ in range(3):
            near = value.astype(jnp.bfloat16).astype(jnp.float32)
            tail = jnp.where(row16 == at, near, tail)
            value = value - near
            at += 1
    shared[z, y, orients : orients + 16, :] = tail.astype(jnp.bfloat16)
    gather(shared, post_send, post_recv)
    for j in range(2, pieces):
        band_relay(j)
    band_finish()
    for d in range(1, classes):
        proj_copy(d, mod(cls + d, classes), cls).wait_send()
        stat_copy(d, cls).wait_send()
    for j in range(NX):
        pair_copy(j).wait_send()
        if j:
            far_copy(j, j).wait_send()


def exchange(mine, projection, weight, prior, slots, col):
    img_rows, wide = mine.shape
    orients, freqs = projection.shape
    width = weight.shape[1]
    dma = pltpu.SemaphoreType.DMA
    classes = 2 * NX
    pieces = 4
    messages = NZ + NZ * NY
    block = (NX, orients, slots)
    vmem = pl.BlockSpec(memory_space=pltpu.VMEM)
    return pl.pallas_call(
        exchange_kernel,
        out_shape=(
            jax.ShapeDtypeStruct((NZ, NY, orients + 16, slots), jnp.bfloat16),
            jax.ShapeDtypeStruct((NZ, NY, NY * NZ, TILE), jnp.bfloat16),
            jax.ShapeDtypeStruct((NZ, NY, img_rows, col), jnp.bfloat16),
        ),
        in_specs=[vmem, pl.BlockSpec(memory_space=pl.ANY), vmem, vmem],
        out_specs=(vmem, vmem, vmem),
        scratch_shapes=[
            pltpu.VMEM((NZ, NY, img_rows, wide), jnp.bfloat16),
            pltpu.VMEM((classes, orients, width), jnp.bfloat16),
            pltpu.VMEM((slots, width), jnp.bfloat16),
            pltpu.VMEM(block, jnp.float32),
            pltpu.VMEM(block, jnp.float32),
            pltpu.VMEM(block, jnp.float32),
            pltpu.VMEM(block, jnp.float32),
            pltpu.VMEM((classes, 8, slots), jnp.float32),
            dma((3,)),
            dma((classes,)),
            dma((classes,)),
            dma((messages,)),
            dma((messages,)),
            dma((messages,)),
            dma((messages,)),
            dma((NX,)),
            dma((NX,)),
            dma((NX,)),
            dma((NX,)),
            dma((classes,)),
            dma((classes,)),
            dma((3, pieces)),
            dma((pieces,)),
        ],
        compiler_params=pltpu.CompilerParams(
            collective_id=0, has_side_effects=True, vmem_limit_bytes=60 * 1024 * 1024
        ),
        name="exchange",
    )(mine, projection, weight, prior)


def sums_kernel(shared, ranks, band, out, evidence, top, full, share, packed):
    owners, total_rows, slots = shared.shape
    orients = out.shape[0]
    img_rows = TILE // 2
    cap = slots // owners
    group = 4
    lanes = group * img_rows

    @pl.when(pl.program_id(0) == 0)
    def _():
        def collect(o, carry):
            tail = shared[o, orients : orients + 16, :].astype(jnp.float32)
            top[pl.ds(o, 1), :] = tail[0:1] + tail[1:2] + tail[2:3]
            full[pl.ds(o, 1), :] = tail[3:4] + tail[4:5] + tail[5:6]
            return carry

        lax.fori_loop(0, owners, collect, 0)
        half = lax.broadcasted_iota(jnp.int32, (owners, TILE), 1) < img_rows
        for q in range(owners // 2):
            rank = jnp.where(half, ranks[2 * q].astype(jnp.float32), ranks[2 * q + 1].astype(jnp.float32))
            rank = rank.astype(jnp.int32)
            named = rank >= 0
            spot = jnp.maximum(rank, 0) + jnp.where(half, 2 * q * cap, (2 * q + 1) * cap)
            first, last = 2 * q * cap // TILE, (2 * (q + 1) * cap - 1) // TILE

            def look(ref):
                found = jnp.zeros((owners, TILE), jnp.float32)
                for t in range(first, last + 1):
                    local = spot - t * TILE
                    inside = jnp.logical_and(local >= 0, local < TILE)
                    value = jnp.take_along_axis(
                        ref[:, t * TILE : (t + 1) * TILE], jnp.clip(local, 0, TILE - 1), axis=1
                    )
                    found = jnp.where(inside, value, found)
                return found

            tops = jnp.where(named, look(top), SENTINEL)
            best = jnp.max(tops, axis=0, keepdims=True)
            raised = jnp.where(named, jnp.exp(tops - best), 0.0)
            amount = jnp.sum(raised * jnp.where(named, look(full), 0.0), axis=0, keepdims=True)
            evidence[q : q + 1, :] = best + jnp.log(amount)
            part = raised / amount
            lane = slice((q % 2) * TILE, (q % 2 + 1) * TILE)
            share[q // 2, 0, :, lane] = jnp.where(named, rank, -1).astype(jnp.float32)
            share[q // 2, 1, :, lane] = part

        row_id = lax.broadcasted_iota(jnp.int32, (group * cap, lanes), 0)
        lane_src = lax.broadcasted_iota(jnp.int32, (group * cap, lanes), 1) // img_rows
        same = lane_src == row_id // cap
        place = jnp.where(same, (row_id % cap).astype(jnp.float32), -2.0)

        def pack(g, carry):
            data = band[pl.ds(pl.multiple_of(g * lanes, lanes), lanes), :]
            blocks = 8
            for b in range(owners // blocks):
                picks = []
                for o in range(b * blocks, (b + 1) * blocks):
                    line = share[g, 0, o : o + 1, :]
                    factor = share[g, 1, o : o + 1, :]
                    picks.append(jnp.where(place == line, factor, 0.0).astype(jnp.bfloat16))
                found = jnp.dot(
                    jnp.concatenate(picks, axis=0), data, preferred_element_type=jnp.float32
                ).astype(jnp.bfloat16)
                for i in range(blocks):
                    packed[b * blocks + i, pl.ds(pl.multiple_of(g * group * cap, 16), group * cap), :] = found[
                        i * group * cap : (i + 1) * group * cap
                    ]
            return carry

        lax.fori_loop(0, owners // group, pack, 0)

    o = pl.program_id(0)
    out[...] = jnp.dot(shared[o, 0:orients, :], packed[o], preferred_element_type=jnp.float32).astype(out.dtype)


def sums(shared, ranks, band, orients):
    owners, total_rows, slots = shared.shape
    images, col = band.shape
    whole = lambda *shape: pl.BlockSpec(shape, lambda o: (0,) * len(shape), pipeline_mode=pl.Buffered(1))
    return pl.pallas_call(
        sums_kernel,
        grid=(owners,),
        out_shape=(
            jax.ShapeDtypeStruct((owners * orients, col), jnp.bfloat16),
            jax.ShapeDtypeStruct((owners // 2, TILE), jnp.float32),
        ),
        in_specs=[whole(*shared.shape), whole(*ranks.shape), whole(*band.shape)],
        out_specs=(pl.BlockSpec((orients, col), lambda o: (o, 0)), pl.BlockSpec((owners // 2, TILE), lambda o: (0, 0))),
        scratch_shapes=[
            pltpu.VMEM((owners, slots), jnp.float32),
            pltpu.VMEM((owners, slots), jnp.float32),
            pltpu.VMEM((owners // 4, 2, owners, 2 * TILE), jnp.float32),
            pltpu.VMEM((owners, slots, col), jnp.bfloat16),
        ],
        compiler_params=pltpu.CompilerParams(
            dimension_semantics=("arbitrary",), vmem_limit_bytes=60 * 1024 * 1024
        ),
        name="sums",
    )(shared, ranks, band)


def body(images, projections, log_prior, significant, shell_index, noise_inv):
    owners = lax.axis_size("ori")
    classes = lax.axis_size("cls")
    own = lax.axis_index("ori")
    cls = lax.axis_index("cls")
    rows, width = images.shape
    listed = significant.shape[1]
    cap = max(2, 3 * rows * listed // (2 * owners))
    slots = owners * cap
    part = width // classes
    col = width // owners
    orients = projections.shape[1]

    shells = lax.dynamic_slice(shell_index, (cls * part,), (part,))
    weight = shell_weights(noise_inv, shells)
    mine = lax.dynamic_slice(images, (0, cls * part), (rows, part))
    mine = (mine.astype(jnp.float32) * weight[None, :]).astype(jnp.bfloat16)
    blocks = jnp.arange(owners, dtype=jnp.int32)
    named = jnp.any(significant[:, :, None] == blocks[None, None, :], axis=1)
    named_int = named.astype(jnp.int32)
    ranks = jnp.where(named, jnp.cumsum(named_int, axis=0) - named_int, -1)
    ranks = ranks.T.astype(jnp.bfloat16)
    ranks = jnp.concatenate([ranks, ranks], axis=1)
    ranks = jnp.concatenate([ranks, jnp.zeros((rows - owners, TILE), jnp.bfloat16)], axis=0)
    mine = jnp.concatenate([mine, ranks], axis=1)
    shared, every_rank, band = exchange(
        mine, projections[0], weight[None, :], log_prior[0][:, None], slots, col
    )
    class_sums, evidence = sums(
        shared.reshape(owners, orients + 16, slots),
        every_rank.reshape(owners, owners, TILE),
        band.reshape(owners * rows, col),
        orients,
    )
    log_evidence = lax.dynamic_slice(evidence.reshape(owners, rows), (own, 0), (1, rows))[0]
    return (class_sums[None], log_evidence)


def solution(mesh):
    in_specs = (P("ori", None), P("cls", "ori", None), P("cls", "ori"), P("ori", None), P(), P())
    out_specs = (P("cls", None, "ori"), P("ori"))
    return jax.shard_map(body, mesh=mesh, in_specs=in_specs, out_specs=out_specs, check_vma=False)
```

```python
import jax
import jax.numpy as jnp
from jax import lax
from jax.experimental import pallas as pl
from jax.experimental.pallas import tpu as pltpu
from jax.sharding import PartitionSpec as P

MESH = pl.DeviceIdType.MESH
SENTINEL = -1e30
TILE = 128
NY = 4
NZ = 8
NX = 4


def mod(value, size):
    return lax.rem(value + size, size)


class Ring:
    def __init__(self, buf, view, pos, sizes, devs, send_sem, recv_sem):
        self.buf, self.view, self.pos, self.sizes, self.devs = buf, view, pos, sizes, devs
        self.send_sem, self.recv_sem = send_sem, recv_sem
        self.started = []
        nf = sizes[0]
        offsets = [0]
        for r in range(1, nf // 2):
            offsets += [-r, r]
        offsets.append(nf // 2)
        self.offsets = offsets

    def copy(self, ident, df, dg, n, r, d, ring):
        (f, g), (nf, ng) = self.pos, self.sizes
        half = d if r == n // 2 - 1 else None
        ref = self.view(self.buf, mod(f + df, nf), mod(g + dg, ng), half)
        return pltpu.make_async_remote_copy(
            src_ref=ref,
            dst_ref=ref,
            send_sem=self.send_sem.at[ident],
            recv_sem=self.recv_sem.at[ident],
            device_id=self.devs[ring](1 - 2 * d),
            device_id_type=MESH,
        )

    def send(self, *what):
        self.copy(*what).start()
        self.started.append(what)

    def f_what(self, r, d, hop):
        return (2 * r + d, -(1 - 2 * d) * (r + hop), 0, self.sizes[0], r, d, 0)

    def g_what(self, j, r, d, hop):
        nf, ng = self.sizes
        return (nf + (j * (ng // 2) + r) * 2 + d, self.offsets[j], -(1 - 2 * d) * (r + hop), ng, r, d, 1)

    def start(self):
        for d in (0, 1):
            self.send(*self.f_what(0, d, 0))
            self.send(*self.g_what(0, 0, d, 0))

    def f_rounds(self):
        return self.sizes[0] // 2

    def f_round(self, r):
        nf = self.sizes[0]
        for d in (0, 1):
            self.copy(*self.f_what(r, d, 1)).wait_recv()
            if r + 1 < nf // 2:
                self.send(*self.f_what(r + 1, d, 0))
        for j in (2 * r + 1, 2 * r + 2):
            if j < nf:
                for d in (0, 1):
                    self.send(*self.g_what(j, 0, d, 0))

    def g_step(self, i):
        nf, ng = self.sizes
        r, j = i // nf, i % nf
        for d in (0, 1):
            self.copy(*self.g_what(j, r, d, 1)).wait_recv()
            if r + 1 < ng // 2:
                self.send(*self.g_what(j, r + 1, d, 0))

    def finish(self):
        for what in self.started:
            self.copy(*what).wait_send()


def lines_of(top, full):
    row = lax.broadcasted_iota(jnp.int32, (8, TILE), 0)
    out = jnp.zeros((8, TILE), jnp.float32)
    at = 0
    for value in (top, full):
        for t in range(value.shape[1] // TILE):
            out = jnp.where(row == at, value[:, t * TILE : (t + 1) * TILE], out)
            at += 1
    return out


def step_kernel(
    img_ref,
    proj_ref,
    prior_ref,
    listed_ref,
    shell_ref,
    noise_ref,
    shared,
    packed,
    evidence_ref,
    evidence,
    weights,
    images,
    proj,
    norms,
    received,
    part,
    from_pair,
    summed,
    from_far,
    stat,
    spread,
    band,
    ranks,
    tops,
    share,
    own_sem,
    proj_send,
    proj_recv,
    img_send,
    img_recv,
    post_send,
    post_recv,
    pair_send,
    pair_recv,
    far_send,
    far_recv,
    stat_send,
    stat_recv,
    spread_send,
    spread_recv,
    band_send,
    band_recv,
):
    cls = lax.axis_index("cls")
    ori = lax.axis_index("ori")
    x, core = cls // 2, cls % 2
    z, y = ori // NY, ori % NY
    classes = 2 * NX
    owners = NY * NZ
    img_rows = images.shape[2]
    width = proj.shape[2]
    col = band.shape[3]
    slots = received.shape[0]
    orients = proj.shape[1]
    cap = slots // owners
    tiles = slots // TILE

    def slot_of(k):
        return (k % 2) * NX + k // 2

    def peer(d, sign):
        c = (core + d) % 2
        return mod(x + sign * (d // 2), NX) * 2 + c

    def cls_dev(k):
        return (k, ori)

    def y_dev(step):
        return (cls, z * NY + mod(y + step, NY))

    def z_dev(step):
        return (cls, mod(z + step, NZ) * NY + y)

    barrier = pltpu.get_barrier_semaphore()
    greeted = [cls_dev(peer(d, 1)) for d in range(1, classes)]
    greeted += [y_dev(d) for d in range(1, NY)]
    greeted += [z_dev(d) for d in range(1, NZ)]
    for dev in greeted:
        pl.semaphore_signal(barrier, inc=1, device_id=dev, device_id_type=MESH)
    own_img = pltpu.make_async_copy(
        img_ref.at[:, pl.ds(pl.multiple_of(cls * width, TILE), width)], received.at[0:img_rows], own_sem.at[0]
    )
    own_img.start()
    own_proj = pltpu.make_async_copy(
        proj_ref.at[:, pl.ds(pl.multiple_of(cls * width, TILE), width)], proj.at[slot_of(cls)], own_sem.at[1]
    )
    own_proj.start()
    shells = shell_ref[...]
    level = jnp.zeros(shells.shape, jnp.float32)
    for j in range(noise_ref.shape[0]):
        level = jnp.where(shells == j, noise_ref[j], level)
    weights[...] = level
    named = jnp.zeros((owners, img_rows), jnp.bool_)
    block_row = lax.broadcasted_iota(jnp.int32, (owners, img_rows), 0)
    for j in range(listed_ref.shape[0]):
        named = jnp.logical_or(named, listed_ref[j : j + 1, :] == block_row)
    named = jnp.where(named, 1.0, 0.0).astype(jnp.bfloat16)
    image_row = lax.broadcasted_iota(jnp.int32, (img_rows, TILE), 0)
    image_lane = lax.broadcasted_iota(jnp.int32, (img_rows, TILE), 1) % img_rows
    twice = jnp.where(image_row == image_lane, 1.0, 0.0).astype(jnp.bfloat16)
    before = jnp.where(image_row < image_lane, 1.0, 0.0).astype(jnp.bfloat16)
    there = jnp.dot(named, twice, preferred_element_type=jnp.float32)
    rank = jnp.dot(named, before, preferred_element_type=jnp.float32)
    rank = jnp.where(there > 0.5, rank, -1.0)
    rank = jnp.concatenate([rank, jnp.zeros((img_rows - owners, TILE), jnp.float32)], axis=0)
    images[z, y, :, width : width + TILE] = rank.astype(jnp.bfloat16)

    def weight_row(j):
        return weights[pl.ds(cls * (width // TILE) + j, 1), :]

    pl.semaphore_wait(barrier, len(greeted))

    def proj_copy(d, to, frm):
        return pltpu.make_async_remote_copy(
            src_ref=proj_ref.at[:, pl.ds(pl.multiple_of(to * width, TILE), width)],
            dst_ref=proj.at[slot_of(frm)],
            send_sem=proj_send.at[d],
            recv_sem=proj_recv.at[d],
            device_id=cls_dev(to),
            device_id_type=MESH,
        )

    for d in (2, 3, 6, 7, 4, 5, 1):
        proj_copy(d, peer(d, 1), cls).start()
    own_img.wait()
    for j in range(width // TILE):
        lane = slice(j * TILE, (j + 1) * TILE)
        images[z, y, :, lane] = (received[0:img_rows, lane].astype(jnp.float32) * weight_row(j)).astype(jnp.bfloat16)

    def slice_view(swap):
        def view(buf, fi, gi, half):
            zi, yi = (fi, gi) if swap else (gi, fi)
            n = buf.shape[2]
            if half is None:
                return buf.at[zi, yi]
            return buf.at[zi, yi, pl.ds(half * (n // 2), n // 2)]

        return view

    def gather(buf, send_sem, recv_sem, f_hooks, g_hooks):
        rings = (
            Ring(buf, slice_view(False), (y, z), (NY, NZ), (y_dev, z_dev), send_sem, recv_sem),
            Ring(buf, slice_view(True), (z, y), (NZ, NY), (z_dev, y_dev), send_sem, recv_sem),
        )

        def both(act):
            for c in range(2):

                @pl.when(core == c)
                def _():
                    act(rings[c])

        both(lambda ring: ring.start())
        for r in range(NZ // 2):
            both(lambda ring: ring.f_round(r) if r < ring.f_rounds() else None)
            for hook in f_hooks.get(r, ()):
                hook()
        for i in range(NY * NZ // 2):
            both(lambda ring: ring.g_step(i))
            for hook in g_hooks.get(i, ()):
                hook()
        both(lambda ring: ring.finish())

    def norm_of(d):
        def run():
            if d == 0:
                own_proj.wait()
            else:
                proj_copy(d, peer(d, 1), peer(d, -1)).wait_recv()
            at = slot_of(peer(d, -1)) if d else slot_of(cls)
            norm = jnp.zeros((orients, TILE), jnp.float32)
            for j in range(width // TILE):
                lane = slice(j * TILE, (j + 1) * TILE)
                wide = proj[at, :, lane].astype(jnp.float32)
                norm = norm + wide * wide * weight_row(j)
            norms[at] = 0.5 * jnp.sum(norm, axis=1, keepdims=True)

        return run

    order = (0, 1, 2, 3, 6, 7)
    gather(images, img_send, img_recv, {}, {10 + i: [norm_of(d)] for i, d in enumerate(order)})

    owner_x, owner_core = z // 2, z % 2
    role = mod(x - owner_x, NX)
    on_line = core == owner_core
    half = NZ // 2
    band_cols = pl.ds(pl.multiple_of(y * col, TILE), col)
    ahead = (mod(x + 1, NX) * 2 + core, ori)
    behind = (mod(x - 1, NX) * 2 + core, ori)
    pair = (x * 2 + 1 - core, ori)
    is_owner = jnp.logical_and(on_line, role == 0)

    def band_copy(j, lane, first):
        return pltpu.make_async_remote_copy(
            src_ref=images.at[j, :, :, band_cols] if first else band.at[j],
            dst_ref=band.at[j],
            send_sem=band_send.at[lane, j],
            recv_sem=band_recv.at[j],
            device_id=(ahead, behind, pair)[lane],
            device_id_type=MESH,
        )

    own_band = pltpu.make_async_copy(images.at[:, :, :, band_cols], band, own_sem.at[2])

    def band_first(js):
        @pl.when(is_owner)
        def _():
            for j in js:
                band_copy(j, 0, True).start()
                band_copy(half + j, 1, True).start()
            for j in js:
                band_copy(j, 2, True).start()
                band_copy(half + j, 2, True).start()

    def relay_plan(s):
        near, mid, far = s - 1, s - 2, s - 3
        plan = {1: [], 2: [], 3: []}
        if 0 <= near < half:
            plan[1].append((near, 0))
            plan[3].append((half + near, 1))
        if 0 <= mid < half:
            plan[2] += [(mid, 0), (half + mid, 1)]
        if 0 <= far < half:
            plan[1].append((half + far, None))
            plan[3].append((far, None))
        return plan

    def band_step(s):
        def run():
            for k, todo in relay_plan(s).items():

                @pl.when(jnp.logical_and(on_line, role == k))
                def _():
                    for j, lane in todo:
                        band_copy(j, 2, False).wait_recv()
                        if lane is not None:
                            band_copy(j, lane, False).start()
                        band_copy(j, 2, False).start()

        return run

    def nth_piece(n):
        return jnp.where(
            role == 3, (n + half) % NZ, jnp.where(role == 2, (n % 2) * half + n // 2, n)
        )

    def band_sent():
        @pl.when(is_owner)
        def _():
            for j in range(half):
                band_copy(j, 0, True).wait_send()
                band_copy(half + j, 1, True).wait_send()
            for j in range(NZ):
                band_copy(j, 2, True).wait_send()

        for k in (1, 2, 3):

            @pl.when(jnp.logical_and(on_line, role == k))
            def _():
                for s in range(1, half + 3):
                    for j, lane in relay_plan(s)[k]:
                        if lane is not None:
                            band_copy(j, lane, False).wait_send()
                        band_copy(j, 2, False).wait_send()

    @pl.when(is_owner)
    def _():
        own_band.start()

    band_first((0, 1))

    lanes = NY * img_rows
    lane_src = lax.broadcasted_iota(jnp.int32, (NY * cap, lanes), 1) // img_rows
    row_id = lax.broadcasted_iota(jnp.int32, (NY * cap, lanes), 0)
    place = jnp.where(lane_src == row_id // cap, (row_id % cap).astype(jnp.float32), -2.0)
    o_row = lax.broadcasted_iota(jnp.int32, (owners, TILE), 0) == ori
    low = lax.broadcasted_iota(jnp.int32, (owners, TILE), 1) < img_rows

    def pick_rows(zi, carry):
        tables = [
            images[zi, yi, 0:owners, width : width + TILE].astype(jnp.float32) for yi in range(NY)
        ]
        both = [jnp.where(low, tables[0], tables[1]), jnp.where(low, tables[2], tables[3])]
        for h in range(2):
            ranks[zi, :, h * TILE : (h + 1) * TILE] = both[h]
        line = jnp.concatenate(
            [jnp.sum(jnp.where(o_row, both[h], 0.0), axis=0, keepdims=True) for h in range(2)], axis=1
        )
        pick = jnp.where(place == line, 1.0, 0.0).astype(jnp.bfloat16)
        data = images[zi, :, :, 0:width].reshape(lanes, width)
        found = jnp.dot(pick, data, preferred_element_type=jnp.float32)
        received[pl.ds(pl.multiple_of(zi * NY * cap, 16), NY * cap), :] = found.astype(jnp.bfloat16)
        return carry

    lax.fori_loop(0, NZ, pick_rows, 0)
    for d in range(1, classes):
        if d not in order:
            norm_of(d)()

    def pair_copy(j):
        return pltpu.make_async_remote_copy(
            src_ref=part.at[j],
            dst_ref=from_pair.at[j],
            send_sem=pair_send.at[j],
            recv_sem=pair_recv.at[j],
            device_id=pair,
            device_id_type=MESH,
        )

    def far_copy(dx):
        return pltpu.make_async_remote_copy(
            src_ref=summed.at[mod(x + dx, NX)],
            dst_ref=from_far.at[dx],
            send_sem=far_send.at[dx],
            recv_sem=far_recv.at[dx],
            device_id=(mod(x + dx, NX) * 2 + core, ori),
            device_id_type=MESH,
        )

    def partial(c):
        block = proj[pl.ds(c * NX, NX)].reshape(NX * orients, width)
        score = lax.dot_general(block, received[...], (((1,), (1,)), ((), ())), preferred_element_type=jnp.float32)
        return score.reshape(NX, orients, slots) - norms[pl.ds(c * NX, NX)]

    part[...] = partial(1 - core)
    for j in range(NX):
        pair_copy(j).start()
    summed[...] = partial(core)
    for dx in (2, 1, 3):
        j = mod(x + dx, NX)
        pair_copy(j).wait_recv()
        summed[j] = summed[j] + from_pair[j]
        far_copy(dx).start()
    band_step(1)()
    band_first((2, 3))
    pair_copy(x).wait_recv()
    square = (orients, orients)
    diagonal = lax.broadcasted_iota(jnp.int32, square, 0) == lax.broadcasted_iota(jnp.int32, square, 1)
    prior = jnp.sum(jnp.where(diagonal, jnp.broadcast_to(prior_ref[...], square), 0.0), axis=1, keepdims=True)
    total = summed[x] + from_pair[x] + prior
    for dx in range(1, NX):
        far_copy(dx).wait_recv()
        total = total + from_far[dx]
    score = total
    peak = jnp.max(score, axis=0, keepdims=True)
    amount = jnp.sum(jnp.exp(score - peak), axis=0, keepdims=True)
    stat[cls] = lines_of(peak, amount)

    def stat_copy(d, frm):
        return pltpu.make_async_remote_copy(
            src_ref=stat.at[frm],
            dst_ref=stat.at[frm],
            send_sem=stat_send.at[d],
            recv_sem=stat_recv.at[d],
            device_id=cls_dev(peer(d, 1)),
            device_id_type=MESH,
        )

    for d in range(1, classes):
        stat_copy(d, cls).start()
    for d in range(1, classes):
        stat_copy(d, peer(d, -1)).wait_recv()
    top = []
    full = []
    for t in range(tiles):
        best = stat[0, t : t + 1]
        for k in range(1, classes):
            best = jnp.maximum(best, stat[k, t : t + 1])
        whole = jnp.zeros_like(best)
        for k in range(classes):
            whole = whole + stat[k, tiles + t : tiles + t + 1] * jnp.exp(stat[k, t : t + 1] - best)
        top.append(best)
        full.append(whole)
    top = jnp.concatenate(top, axis=1)
    full = jnp.concatenate(full, axis=1)
    spread[z, y] = lines_of(top, full)

    def spread_y(d, yi):
        return pltpu.make_async_remote_copy(
            src_ref=spread.at[z, yi],
            dst_ref=spread.at[z, yi],
            send_sem=spread_send.at[d],
            recv_sem=spread_recv.at[d],
            device_id=y_dev(d),
            device_id_type=MESH,
        )

    def spread_z(d, zi):
        return pltpu.make_async_remote_copy(
            src_ref=spread.at[zi],
            dst_ref=spread.at[zi],
            send_sem=spread_send.at[NY + d],
            recv_sem=spread_recv.at[NY + d],
            device_id=z_dev(d),
            device_id_type=MESH,
        )

    for d in range(1, NY):
        spread_y(d, y).start()
    shared[z, y] = jnp.exp(score - top).astype(jnp.bfloat16)

    def spread_on():
        for d in range(1, NY):
            spread_y(d, mod(y - d, NY)).wait_recv()
        for d in range(1, NZ):
            spread_z(d, z).start()

    def spread_end():
        for d in range(1, NZ):
            spread_z(d, mod(z - d, NZ)).wait_recv()
        for zi in range(NZ):
            for yi in range(NY):
                o = zi * NY + yi
                for t in range(2 * tiles):
                    tops[t, o : o + 1, :] = spread[zi, yi, t : t + 1, :]

    def shares_of(qs):
        def run():
            lanes_of = {q: slice((q % 2) * TILE, (q % 2 + 1) * TILE) for q in qs}
            rank = {q: ranks[q // 2, :, lanes_of[q]].astype(jnp.int32) for q in qs}
            named = {q: rank[q] >= 0 for q in qs}
            spot = {
                q: jnp.maximum(rank[q], 0) + jnp.where(low, 2 * q * cap, (2 * q + 1) * cap) for q in qs
            }

            def look(q, base):
                first, last = 2 * q * cap // TILE, (2 * (q + 1) * cap - 1) // TILE
                found = None
                for t in range(first, last + 1):
                    local = spot[q] - t * TILE
                    value = jnp.take_along_axis(tops[base + t], jnp.clip(local, 0, TILE - 1), axis=1)
                    found = value if found is None else jnp.where(local >= 0, value, found)
                return found

            highs = {q: jnp.where(named[q], look(q, 0), SENTINEL) for q in qs}
            wholes = {q: jnp.where(named[q], look(q, tiles), 0.0) for q in qs}
            best = {q: jnp.max(highs[q], axis=0, keepdims=True) for q in qs}
            raised = {q: jnp.where(named[q], jnp.exp(highs[q] - best[q]), 0.0) for q in qs}
            whole = {q: jnp.sum(raised[q] * wholes[q], axis=0, keepdims=True) for q in qs}
            part_of = {q: raised[q] / whole[q] for q in qs}
            for q in qs:
                share[q // 2, :, lanes_of[q]] = part_of[q]
                evidence[q : q + 1, :] = best[q] + jnp.log(whole[q])

        return run

    def pack(n):
        def run():
            g = nth_piece(n)

            @pl.when(jnp.logical_not(on_line))
            def _():
                band_copy(g, 2, False).wait_recv()

            data = band[g].reshape(lanes, col)
            blocks = 8

            def some(b, carry):
                first = pl.multiple_of(b * blocks, blocks)
                table = ranks[g, pl.ds(first, blocks), :]
                factor = share[g, pl.ds(first, blocks), :]
                picks = [
                    jnp.where(place == table[i : i + 1], factor[i : i + 1], 0.0).astype(jnp.bfloat16)
                    for i in range(blocks)
                ]
                found = jnp.dot(
                    jnp.concatenate(picks, axis=0), data, preferred_element_type=jnp.float32
                ).astype(jnp.bfloat16)
                packed[pl.ds(first, blocks), pl.ds(pl.multiple_of(g * NY * cap, 16), NY * cap), :] = found.reshape(
                    blocks, NY * cap, col
                )
                return carry

            lax.fori_loop(0, owners // blocks, some, 0)

        return run

    def quarter(n):
        return shares_of(range(n * 4, n * 4 + 4))

    hooks = {
        0: [spread_end],
        1: [band_step(3), quarter(0)],
        2: [quarter(1)],
        3: [quarter(2)],
        4: [band_step(4), quarter(3)],
        5: [pack(0)],
        6: [pack(1)],
        7: [band_step(5), pack(2)],
        8: [pack(3)],
        9: [pack(4)],
        10: [band_step(6), pack(5)],
        11: [pack(6)],
        12: [pack(7)],
    }

    @pl.when(is_owner)
    def _():
        own_band.wait()

    gather(shared, post_send, post_recv, {0: [spread_on, band_step(2)]}, hooks)

    line = evidence[pl.ds(ori // 2, 1), :]
    other = pltpu.roll(line, img_rows, 1)
    evidence_ref[...] = jnp.where(ori % 2 == 0, line, other)[:, 0:img_rows]
    band_sent()
    for d in range(1, classes):
        proj_copy(d, peer(d, 1), cls).wait_send()
        stat_copy(d, cls).wait_send()
    for j in range(NX):
        pair_copy(j).wait_send()
        if j:
            far_copy(j).wait_send()
    for d in range(1, NY):
        spread_y(d, y).wait_send()
    for d in range(1, NZ):
        spread_z(d, z).wait_send()


def step(images, projection, prior, listed, shells, noise, slots, col):
    img_rows, freqs = images.shape
    orients = projection.shape[0]
    width = freqs // (2 * NX)
    wide = width + TILE
    owners = NY * NZ
    dma = pltpu.SemaphoreType.DMA
    classes = 2 * NX
    messages = NZ + NZ * NY
    block = (NX, orients, slots)
    vmem = pl.BlockSpec(memory_space=pltpu.VMEM)
    bf16, f32 = jnp.bfloat16, jnp.float32
    return pl.pallas_call(
        step_kernel,
        out_shape=(
            jax.ShapeDtypeStruct((NZ, NY, orients, slots), bf16),
            jax.ShapeDtypeStruct((owners, slots, col), bf16),
            jax.ShapeDtypeStruct((1, img_rows), f32),
        ),
        in_specs=[
            pl.BlockSpec(memory_space=pltpu.HBM),
            pl.BlockSpec(memory_space=pltpu.HBM),
            vmem,
            vmem,
            vmem,
            pl.BlockSpec(memory_space=pltpu.SMEM),
        ],
        out_specs=(vmem, vmem, vmem),
        scratch_shapes=[
            pltpu.VMEM((owners // 2, TILE), f32),
            pltpu.VMEM(shells.shape, f32),
            pltpu.VMEM((NZ, NY, img_rows, wide), bf16),
            pltpu.VMEM((classes, orients, width), bf16),
            pltpu.VMEM((classes, orients, 1), f32),
            pltpu.VMEM((slots, width), bf16),
            pltpu.VMEM(block, f32),
            pltpu.VMEM(block, f32),
            pltpu.VMEM(block, f32),
            pltpu.VMEM(block, f32),
            pltpu.VMEM((classes, 8, TILE), f32),
            pltpu.VMEM((NZ, NY, 8, TILE), f32),
            pltpu.VMEM((NZ, NY, img_rows, col), bf16),
            pltpu.VMEM((NZ, owners, 2 * TILE), f32),
            pltpu.VMEM((8, owners, TILE), f32),
            pltpu.VMEM((NZ, owners, 2 * TILE), f32),
            dma((3,)),
            dma((classes,)),
            dma((classes,)),
            dma((messages,)),
            dma((messages,)),
            dma((messages,)),
            dma((messages,)),
            dma((NX,)),
            dma((NX,)),
            dma((NX,)),
            dma((NX,)),
            dma((classes,)),
            dma((classes,)),
            dma((NY + NZ,)),
            dma((NY + NZ,)),
            dma((3, NZ)),
            dma((NZ,)),
        ],
        compiler_params=pltpu.CompilerParams(
            collective_id=0, has_side_effects=True, vmem_limit_bytes=28 * 1024 * 1024
        ),
        name="estep",
    )(images, projection, prior, listed, shells, noise)


def sums_kernel(shared, packed, out_ref, stage, out_sem):
    owners = packed.shape[0]
    orients = shared.shape[2]

    def out_copy(o, s):
        return pltpu.make_async_copy(
            stage.at[s], out_ref.at[pl.ds(pl.multiple_of(o * orients, 16), orients), :], out_sem.at[s]
        )

    depth = stage.shape[0] // 2

    def emit(t, carry):
        base = lax.rem(t, 2) * depth

        @pl.when(t > 1)
        def _():
            for s in range(depth):
                out_copy((t - 2) * depth + s, base + s).wait()

        for s in range(depth):
            o = t * depth + s
            stage[base + s] = jnp.dot(
                shared[o // NY, o % NY], packed[o], preferred_element_type=jnp.float32
            ).astype(jnp.bfloat16)
        for s in range(depth):
            out_copy(t * depth + s, base + s).start()
        return carry

    rounds = owners // depth
    lax.fori_loop(0, rounds, emit, 0)
    for t in (rounds - 2, rounds - 1):
        for s in range(depth):
            out_copy(t * depth + s, (t % 2) * depth + s).wait()


def sums(shared, packed):
    owners, slots, col = packed.shape
    orients = shared.shape[2]
    vmem = pl.BlockSpec(memory_space=pltpu.VMEM)
    return pl.pallas_call(
        sums_kernel,
        out_shape=jax.ShapeDtypeStruct((owners * orients, col), jnp.bfloat16),
        in_specs=[vmem, vmem],
        out_specs=pl.BlockSpec(memory_space=pltpu.HBM),
        scratch_shapes=[pltpu.VMEM((8, orients, col), jnp.bfloat16), pltpu.SemaphoreType.DMA((8,))],
        compiler_params=pltpu.CompilerParams(vmem_limit_bytes=8 * 1024 * 1024),
        name="sums",
    )(shared, packed)


def body(images, projections, log_prior, significant, shell_index, noise_inv):
    owners = lax.axis_size("ori")
    rows, width = images.shape
    listed = significant.shape[1]
    cap = max(2, 3 * rows * listed // (2 * owners))
    shared, packed, evidence = step(
        pltpu.with_memory_space_constraint(images, pltpu.HBM),
        pltpu.with_memory_space_constraint(projections[0], pltpu.HBM),
        log_prior,
        significant.T,
        shell_index.reshape(width // TILE, TILE),
        noise_inv,
        owners * cap,
        width // owners,
    )
    return (sums(shared, packed)[None], evidence[0])


def solution(mesh):
    in_specs = (P("ori", None), P("cls", "ori", None), P("cls", "ori"), P("ori", None), P(), P())
    out_specs = (P("cls", None, "ori"), P("ori"))
    return jax.shard_map(body, mesh=mesh, in_specs=in_specs, out_specs=out_specs, check_vma=False)
```

```python
import jax
import jax.numpy as jnp
from jax import lax
from jax.experimental import pallas as pl
from jax.experimental.pallas import tpu as pltpu
from jax.sharding import PartitionSpec as P

MESH = pl.DeviceIdType.MESH
SENTINEL = -1e30
TILE = 128
NY = 4
NZ = 8
NX = 4


def mod(value, size):
    return lax.rem(value + size, size)


class Ring:
    def __init__(self, buf, view, pos, sizes, devs, send_sem, recv_sem):
        self.buf, self.view, self.pos, self.sizes, self.devs = buf, view, pos, sizes, devs
        self.send_sem, self.recv_sem = send_sem, recv_sem
        self.started = []
        nf = sizes[0]
        offsets = [0]
        for r in range(1, nf // 2):
            offsets += [-r, r]
        offsets.append(nf // 2)
        self.offsets = offsets

    def copy(self, ident, df, dg, n, r, d, ring):
        (f, g), (nf, ng) = self.pos, self.sizes
        half = d if r == n // 2 - 1 else None
        ref = self.view(self.buf, mod(f + df, nf), mod(g + dg, ng), half)
        return pltpu.make_async_remote_copy(
            src_ref=ref,
            dst_ref=ref,
            send_sem=self.send_sem.at[ident],
            recv_sem=self.recv_sem.at[ident],
            device_id=self.devs[ring](1 - 2 * d),
            device_id_type=MESH,
        )

    def send(self, *what):
        self.copy(*what).start()
        self.started.append(what)

    def f_what(self, r, d, hop):
        return (2 * r + d, -(1 - 2 * d) * (r + hop), 0, self.sizes[0], r, d, 0)

    def g_what(self, j, r, d, hop):
        nf, ng = self.sizes
        return (nf + (j * (ng // 2) + r) * 2 + d, self.offsets[j], -(1 - 2 * d) * (r + hop), ng, r, d, 1)

    def start(self):
        for d in (0, 1):
            self.send(*self.f_what(0, d, 0))
            self.send(*self.g_what(0, 0, d, 0))

    def f_rounds(self):
        return self.sizes[0] // 2

    def f_round(self, r):
        nf = self.sizes[0]
        for d in (0, 1):
            self.copy(*self.f_what(r, d, 1)).wait_recv()
            if r + 1 < nf // 2:
                self.send(*self.f_what(r + 1, d, 0))
        for j in (2 * r + 1, 2 * r + 2):
            if j < nf:
                for d in (0, 1):
                    self.send(*self.g_what(j, 0, d, 0))

    def g_step(self, i):
        nf, ng = self.sizes
        r, j = i // nf, i % nf
        for d in (0, 1):
            self.copy(*self.g_what(j, r, d, 1)).wait_recv()
            if r + 1 < ng // 2:
                self.send(*self.g_what(j, r + 1, d, 0))

    def finish(self):
        for what in self.started:
            self.copy(*what).wait_send()


def lines_of(top, full):
    row = lax.broadcasted_iota(jnp.int32, (8, TILE), 0)
    out = jnp.zeros((8, TILE), jnp.float32)
    at = 0
    for value in (top, full):
        for t in range(value.shape[1] // TILE):
            out = jnp.where(row == at, value[:, t * TILE : (t + 1) * TILE], out)
            at += 1
    return out


def step_kernel(
    img_ref,
    proj_ref,
    prior_in,
    listed_in,
    shell_in,
    noise_ref,
    shared,
    packed,
    evidence_ref,
    prior_ref,
    listed_ref,
    shell_ref,
    evidence,
    weights,
    images,
    proj,
    norms,
    received,
    part,
    from_pair,
    summed,
    from_far,
    stat,
    spread,
    band,
    ranks,
    tops,
    share,
    own_sem,
    proj_send,
    proj_recv,
    img_send,
    img_recv,
    post_send,
    post_recv,
    pair_send,
    pair_recv,
    far_send,
    far_recv,
    stat_send,
    stat_recv,
    spread_send,
    spread_recv,
    band_send,
    band_recv,
):
    cls = lax.axis_index("cls")
    ori = lax.axis_index("ori")
    x, core = cls // 2, cls % 2
    z, y = ori // NY, ori % NY
    classes = 2 * NX
    owners = NY * NZ
    img_rows = images.shape[2]
    width = proj.shape[2]
    col = band.shape[3]
    slots = received.shape[0]
    orients = proj.shape[1]
    cap = slots // owners
    tiles = slots // TILE

    def slot_of(k):
        return (k % 2) * NX + k // 2

    def peer(d, sign):
        c = (core + d) % 2
        return mod(x + sign * (d // 2), NX) * 2 + c

    def cls_dev(k):
        return (k, ori)

    def y_dev(step):
        return (cls, z * NY + mod(y + step, NY))

    def z_dev(step):
        return (cls, mod(z + step, NZ) * NY + y)

    small = [
        pltpu.make_async_copy(src, dst, own_sem.at[3 + i])
        for i, (src, dst) in enumerate(((shell_in, shell_ref), (listed_in, listed_ref), (prior_in, prior_ref)))
    ]
    for cp in small:
        cp.start()
    barrier = pltpu.get_barrier_semaphore()
    greeted = [cls_dev(peer(d, 1)) for d in range(1, classes)]
    greeted += [y_dev(d) for d in range(1, NY)]
    greeted += [z_dev(d) for d in range(1, NZ)]
    for dev in greeted:
        pl.semaphore_signal(barrier, inc=1, device_id=dev, device_id_type=MESH)
    own_img = pltpu.make_async_copy(
        img_ref.at[:, pl.ds(pl.multiple_of(cls * width, TILE), width)], received.at[0:img_rows], own_sem.at[0]
    )
    own_img.start()
    own_proj = pltpu.make_async_copy(
        proj_ref.at[:, pl.ds(pl.multiple_of(cls * width, TILE), width)], proj.at[slot_of(cls)], own_sem.at[1]
    )
    own_proj.start()
    for cp in small:
        cp.wait()
    shells = shell_ref[...]
    level = jnp.zeros(shells.shape, jnp.float32)
    for j in range(noise_ref.shape[0]):
        level = jnp.where(shells == j, noise_ref[j], level)
    weights[...] = level
    named = jnp.zeros((owners, img_rows), jnp.bool_)
    block_row = lax.broadcasted_iota(jnp.int32, (owners, img_rows), 0)
    for j in range(listed_ref.shape[0]):
        named = jnp.logical_or(named, listed_ref[j : j + 1, :] == block_row)
    named = jnp.where(named, 1.0, 0.0).astype(jnp.bfloat16)
    image_row = lax.broadcasted_iota(jnp.int32, (img_rows, TILE), 0)
    image_lane = lax.broadcasted_iota(jnp.int32, (img_rows, TILE), 1) % img_rows
    twice = jnp.where(image_row == image_lane, 1.0, 0.0).astype(jnp.bfloat16)
    before = jnp.where(image_row < image_lane, 1.0, 0.0).astype(jnp.bfloat16)
    there = jnp.dot(named, twice, preferred_element_type=jnp.float32)
    rank = jnp.dot(named, before, preferred_element_type=jnp.float32)
    rank = jnp.where(there > 0.5, rank, -1.0)
    rank = jnp.concatenate([rank, jnp.zeros((img_rows - owners, TILE), jnp.float32)], axis=0)
    images[z, y, :, width : width + TILE] = rank.astype(jnp.bfloat16)

    def weight_row(j):
        return weights[pl.ds(cls * (width // TILE) + j, 1), :]

    pl.semaphore_wait(barrier, len(greeted))

    def proj_copy(d, to, frm):
        return pltpu.make_async_remote_copy(
            src_ref=proj_ref.at[:, pl.ds(pl.multiple_of(to * width, TILE), width)],
            dst_ref=proj.at[slot_of(frm)],
            send_sem=proj_send.at[d],
            recv_sem=proj_recv.at[d],
            device_id=cls_dev(to),
            device_id_type=MESH,
        )

    for d in (2, 3, 6, 7, 4, 5, 1):
        proj_copy(d, peer(d, 1), cls).start()
    own_img.wait()
    for j in range(width // TILE):
        lane = slice(j * TILE, (j + 1) * TILE)
        images[z, y, :, lane] = (received[0:img_rows, lane].astype(jnp.float32) * weight_row(j)).astype(jnp.bfloat16)

    def slice_view(swap):
        def view(buf, fi, gi, half):
            zi, yi = (fi, gi) if swap else (gi, fi)
            n = buf.shape[2]
            if half is None:
                return buf.at[zi, yi]
            return buf.at[zi, yi, pl.ds(half * (n // 2), n // 2)]

        return view

    def gather(buf, send_sem, recv_sem, f_hooks, g_hooks):
        rings = (
            Ring(buf, slice_view(False), (y, z), (NY, NZ), (y_dev, z_dev), send_sem, recv_sem),
            Ring(buf, slice_view(True), (z, y), (NZ, NY), (z_dev, y_dev), send_sem, recv_sem),
        )

        def both(act):
            for c in range(2):

                @pl.when(core == c)
                def _():
                    act(rings[c])

        both(lambda ring: ring.start())
        for r in range(NZ // 2):
            both(lambda ring: ring.f_round(r) if r < ring.f_rounds() else None)
            for hook in f_hooks.get(r, ()):
                hook()
        for i in range(NY * NZ // 2):
            both(lambda ring: ring.g_step(i))
            for hook in g_hooks.get(i, ()):
                hook()
        both(lambda ring: ring.finish())

    def norm_of(d):
        def run():
            if d == 0:
                own_proj.wait()
            else:
                proj_copy(d, peer(d, 1), peer(d, -1)).wait_recv()
            at = slot_of(peer(d, -1)) if d else slot_of(cls)
            norm = jnp.zeros((orients, TILE), jnp.float32)
            for j in range(width // TILE):
                lane = slice(j * TILE, (j + 1) * TILE)
                wide = proj[at, :, lane].astype(jnp.float32)
                norm = norm + wide * wide * weight_row(j)
            norms[at] = 0.5 * jnp.sum(norm, axis=1, keepdims=True)

        return run

    order = (0, 1, 2, 3, 6, 7)
    gather(images, img_send, img_recv, {}, {10 + i: [norm_of(d)] for i, d in enumerate(order)})

    owner_x, owner_core = z // 2, z % 2
    role = mod(x - owner_x, NX)
    on_line = core == owner_core
    half = NZ // 2
    band_cols = pl.ds(pl.multiple_of(y * col, TILE), col)
    ahead = (mod(x + 1, NX) * 2 + core, ori)
    behind = (mod(x - 1, NX) * 2 + core, ori)
    pair = (x * 2 + 1 - core, ori)
    is_owner = jnp.logical_and(on_line, role == 0)

    def band_copy(j, lane, first):
        return pltpu.make_async_remote_copy(
            src_ref=images.at[j, :, :, band_cols] if first else band.at[j],
            dst_ref=band.at[j],
            send_sem=band_send.at[lane, j],
            recv_sem=band_recv.at[j],
            device_id=(ahead, behind, pair)[lane],
            device_id_type=MESH,
        )

    own_band = pltpu.make_async_copy(images.at[:, :, :, band_cols], band, own_sem.at[2])

    def band_first(js):
        @pl.when(is_owner)
        def _():
            for j in js:
                band_copy(j, 0, True).start()
                band_copy(half + j, 1, True).start()
            for j in js:
                band_copy(j, 2, True).start()
                band_copy(half + j, 2, True).start()

    def relay_plan(s):
        near, mid, far = s - 1, s - 2, s - 3
        plan = {1: [], 2: [], 3: []}
        if 0 <= near < half:
            plan[1].append((near, 0))
            plan[3].append((half + near, 1))
        if 0 <= mid < half:
            plan[2] += [(mid, 0), (half + mid, 1)]
        if 0 <= far < half:
            plan[1].append((half + far, None))
            plan[3].append((far, None))
        return plan

    def band_step(s):
        def run():
            for k, todo in relay_plan(s).items():

                @pl.when(jnp.logical_and(on_line, role == k))
                def _():
                    for j, lane in todo:
                        band_copy(j, 2, False).wait_recv()
                        if lane is not None:
                            band_copy(j, lane, False).start()
                        band_copy(j, 2, False).start()

        return run

    def nth_piece(n):
        return jnp.where(
            role == 3, (n + half) % NZ, jnp.where(role == 2, (n % 2) * half + n // 2, n)
        )

    def band_sent():
        @pl.when(is_owner)
        def _():
            for j in range(half):
                band_copy(j, 0, True).wait_send()
                band_copy(half + j, 1, True).wait_send()
            for j in range(NZ):
                band_copy(j, 2, True).wait_send()

        for k in (1, 2, 3):

            @pl.when(jnp.logical_and(on_line, role == k))
            def _():
                for s in range(1, half + 3):
                    for j, lane in relay_plan(s)[k]:
                        if lane is not None:
                            band_copy(j, lane, False).wait_send()
                        band_copy(j, 2, False).wait_send()

    @pl.when(is_owner)
    def _():
        own_band.start()

    band_first((0, 1))

    lanes = NY * img_rows
    lane_src = lax.broadcasted_iota(jnp.int32, (NY * cap, lanes), 1) // img_rows
    row_id = lax.broadcasted_iota(jnp.int32, (NY * cap, lanes), 0)
    place = jnp.where(lane_src == row_id // cap, (row_id % cap).astype(jnp.float32), -2.0)
    o_row = lax.broadcasted_iota(jnp.int32, (owners, TILE), 0) == ori
    low = lax.broadcasted_iota(jnp.int32, (owners, TILE), 1) < img_rows

    def pick_rows(zi, carry):
        tables = [
            images[zi, yi, 0:owners, width : width + TILE].astype(jnp.float32) for yi in range(NY)
        ]
        both = [jnp.where(low, tables[0], tables[1]), jnp.where(low, tables[2], tables[3])]
        for h in range(2):
            ranks[zi, :, h * TILE : (h + 1) * TILE] = both[h]
        line = jnp.concatenate(
            [jnp.sum(jnp.where(o_row, both[h], 0.0), axis=0, keepdims=True) for h in range(2)], axis=1
        )
        pick = jnp.where(place == line, 1.0, 0.0).astype(jnp.bfloat16)
        data = images[zi, :, :, 0:width].reshape(lanes, width)
        found = jnp.dot(pick, data, preferred_element_type=jnp.float32)
        received[pl.ds(pl.multiple_of(zi * NY * cap, 16), NY * cap), :] = found.astype(jnp.bfloat16)
        return carry

    lax.fori_loop(0, NZ, pick_rows, 0)
    for d in range(1, classes):
        if d not in order:
            norm_of(d)()

    def pair_copy(j):
        return pltpu.make_async_remote_copy(
            src_ref=part.at[j],
            dst_ref=from_pair.at[j],
            send_sem=pair_send.at[j],
            recv_sem=pair_recv.at[j],
            device_id=pair,
            device_id_type=MESH,
        )

    def far_copy(dx):
        return pltpu.make_async_remote_copy(
            src_ref=summed.at[mod(x + dx, NX)],
            dst_ref=from_far.at[dx],
            send_sem=far_send.at[dx],
            recv_sem=far_recv.at[dx],
            device_id=(mod(x + dx, NX) * 2 + core, ori),
            device_id_type=MESH,
        )

    def partial(c):
        block = proj[pl.ds(c * NX, NX)].reshape(NX * orients, width)
        score = lax.dot_general(block, received[...], (((1,), (1,)), ((), ())), preferred_element_type=jnp.float32)
        return score.reshape(NX, orients, slots) - norms[pl.ds(c * NX, NX)]

    part[...] = partial(1 - core)
    for j in range(NX):
        pair_copy(j).start()
    summed[...] = partial(core)
    for dx in (2, 1, 3):
        j = mod(x + dx, NX)
        pair_copy(j).wait_recv()
        summed[j] = summed[j] + from_pair[j]
        far_copy(dx).start()
    band_step(1)()
    band_first((2, 3))
    pair_copy(x).wait_recv()
    square = (orients, orients)
    diagonal = lax.broadcasted_iota(jnp.int32, square, 0) == lax.broadcasted_iota(jnp.int32, square, 1)
    prior = jnp.sum(jnp.where(diagonal, jnp.broadcast_to(prior_ref[...], square), 0.0), axis=1, keepdims=True)
    total = summed[x] + from_pair[x] + prior
    for dx in range(1, NX):
        far_copy(dx).wait_recv()
        total = total + from_far[dx]
    score = total
    peak = jnp.max(score, axis=0, keepdims=True)
    amount = jnp.sum(jnp.exp(score - peak), axis=0, keepdims=True)
    stat[cls] = lines_of(peak, amount)

    def stat_copy(d, frm):
        return pltpu.make_async_remote_copy(
            src_ref=stat.at[frm],
            dst_ref=stat.at[frm],
            send_sem=stat_send.at[d],
            recv_sem=stat_recv.at[d],
            device_id=cls_dev(peer(d, 1)),
            device_id_type=MESH,
        )

    for d in range(1, classes):
        stat_copy(d, cls).start()
    for d in range(1, classes):
        stat_copy(d, peer(d, -1)).wait_recv()
    top = []
    full = []
    for t in range(tiles):
        best = stat[0, t : t + 1]
        for k in range(1, classes):
            best = jnp.maximum(best, stat[k, t : t + 1])
        whole = jnp.zeros_like(best)
        for k in range(classes):
            whole = whole + stat[k, tiles + t : tiles + t + 1] * jnp.exp(stat[k, t : t + 1] - best)
        top.append(best)
        full.append(whole)
    top = jnp.concatenate(top, axis=1)
    full = jnp.concatenate(full, axis=1)
    spread[z, y] = lines_of(top, full)

    def spread_y(d, yi):
        return pltpu.make_async_remote_copy(
            src_ref=spread.at[z, yi],
            dst_ref=spread.at[z, yi],
            send_sem=spread_send.at[d],
            recv_sem=spread_recv.at[d],
            device_id=y_dev(d),
            device_id_type=MESH,
        )

    def spread_z(d, zi):
        return pltpu.make_async_remote_copy(
            src_ref=spread.at[zi],
            dst_ref=spread.at[zi],
            send_sem=spread_send.at[NY + d],
            recv_sem=spread_recv.at[NY + d],
            device_id=z_dev(d),
            device_id_type=MESH,
        )

    for d in range(1, NY):
        spread_y(d, y).start()
    shared[z, y] = jnp.exp(score - top).astype(jnp.bfloat16)

    def spread_on():
        for d in range(1, NY):
            spread_y(d, mod(y - d, NY)).wait_recv()
        for d in range(1, NZ):
            spread_z(d, z).start()

    def spread_end():
        for d in range(1, NZ):
            spread_z(d, mod(z - d, NZ)).wait_recv()
        for zi in range(NZ):
            for yi in range(NY):
                o = zi * NY + yi
                for t in range(2 * tiles):
                    tops[t, o : o + 1, :] = spread[zi, yi, t : t + 1, :]

    def shares_of(qs):
        def run():
            lanes_of = {q: slice((q % 2) * TILE, (q % 2 + 1) * TILE) for q in qs}
            rank = {q: ranks[q // 2, :, lanes_of[q]].astype(jnp.int32) for q in qs}
            named = {q: rank[q] >= 0 for q in qs}
            spot = {
                q: jnp.maximum(rank[q], 0) + jnp.where(low, 2 * q * cap, (2 * q + 1) * cap) for q in qs
            }

            def look(q, base):
                first, last = 2 * q * cap // TILE, (2 * (q + 1) * cap - 1) // TILE
                found = None
                for t in range(first, last + 1):
                    local = spot[q] - t * TILE
                    value = jnp.take_along_axis(tops[base + t], jnp.clip(local, 0, TILE - 1), axis=1)
                    found = value if found is None else jnp.where(local >= 0, value, found)
                return found

            highs = {q: jnp.where(named[q], look(q, 0), SENTINEL) for q in qs}
            wholes = {q: jnp.where(named[q], look(q, tiles), 0.0) for q in qs}
            best = {q: jnp.max(highs[q], axis=0, keepdims=True) for q in qs}
            raised = {q: jnp.where(named[q], jnp.exp(highs[q] - best[q]), 0.0) for q in qs}
            whole = {q: jnp.sum(raised[q] * wholes[q], axis=0, keepdims=True) for q in qs}
            part_of = {q: raised[q] / whole[q] for q in qs}
            for q in qs:
                share[q // 2, :, lanes_of[q]] = part_of[q]
                evidence[q : q + 1, :] = best[q] + jnp.log(whole[q])

        return run

    def pack(n):
        def run():
            g = nth_piece(n)

            @pl.when(jnp.logical_not(on_line))
            def _():
                band_copy(g, 2, False).wait_recv()

            data = band[g].reshape(lanes, col)
            blocks = 8

            def some(b, carry):
                first = pl.multiple_of(b * blocks, blocks)
                table = ranks[g, pl.ds(first, blocks), :]
                factor = share[g, pl.ds(first, blocks), :]
                picks = [
                    jnp.where(place == table[i : i + 1], factor[i : i + 1], 0.0).astype(jnp.bfloat16)
                    for i in range(blocks)
                ]
                found = jnp.dot(
                    jnp.concatenate(picks, axis=0), data, preferred_element_type=jnp.float32
                ).astype(jnp.bfloat16)
                packed[pl.ds(first, blocks), pl.ds(pl.multiple_of(g * NY * cap, 16), NY * cap), :] = found.reshape(
                    blocks, NY * cap, col
                )
                return carry

            lax.fori_loop(0, owners // blocks, some, 0)

        return run

    def quarter(n):
        return shares_of(range(n * 4, n * 4 + 4))

    hooks = {
        0: [spread_end],
        1: [band_step(3), quarter(0)],
        2: [quarter(1)],
        3: [quarter(2)],
        4: [band_step(4), quarter(3)],
        5: [pack(0)],
        6: [pack(1)],
        7: [band_step(5), pack(2)],
        8: [pack(3)],
        9: [pack(4)],
        10: [band_step(6), pack(5)],
        11: [pack(6)],
        12: [pack(7)],
    }

    @pl.when(is_owner)
    def _():
        own_band.wait()

    gather(shared, post_send, post_recv, {0: [spread_on, band_step(2)]}, hooks)

    line = evidence[pl.ds(ori // 2, 1), :]
    other = pltpu.roll(line, img_rows, 1)
    evidence_ref[...] = jnp.where(ori % 2 == 0, line, other)[:, 0:img_rows]
    band_sent()
    for d in range(1, classes):
        proj_copy(d, peer(d, 1), cls).wait_send()
        stat_copy(d, cls).wait_send()
    for j in range(NX):
        pair_copy(j).wait_send()
        if j:
            far_copy(j).wait_send()
    for d in range(1, NY):
        spread_y(d, y).wait_send()
    for d in range(1, NZ):
        spread_z(d, z).wait_send()


def step(images, projection, prior, listed, shells, noise, slots, col):
    img_rows, freqs = images.shape
    orients = projection.shape[0]
    width = freqs // (2 * NX)
    wide = width + TILE
    owners = NY * NZ
    dma = pltpu.SemaphoreType.DMA
    classes = 2 * NX
    messages = NZ + NZ * NY
    block = (NX, orients, slots)
    vmem = pl.BlockSpec(memory_space=pltpu.VMEM)
    bf16, f32 = jnp.bfloat16, jnp.float32
    return pl.pallas_call(
        step_kernel,
        out_shape=(
            jax.ShapeDtypeStruct((NZ, NY, orients, slots), bf16),
            jax.ShapeDtypeStruct((owners, slots, col), bf16),
            jax.ShapeDtypeStruct((1, img_rows), f32),
        ),
        in_specs=[
            pl.BlockSpec(memory_space=pltpu.HBM),
            pl.BlockSpec(memory_space=pltpu.HBM),
            pl.BlockSpec(memory_space=pltpu.HBM),
            pl.BlockSpec(memory_space=pltpu.HBM),
            pl.BlockSpec(memory_space=pltpu.HBM),
            pl.BlockSpec(memory_space=pltpu.SMEM),
        ],
        out_specs=(vmem, vmem, vmem),
        scratch_shapes=[
            pltpu.VMEM(prior.shape, f32),
            pltpu.VMEM(listed.shape, jnp.int32),
            pltpu.VMEM(shells.shape, jnp.int32),
            pltpu.VMEM((owners // 2, TILE), f32),
            pltpu.VMEM(shells.shape, f32),
            pltpu.VMEM((NZ, NY, img_rows, wide), bf16),
            pltpu.VMEM((classes, orients, width), bf16),
            pltpu.VMEM((classes, orients, 1), f32),
            pltpu.VMEM((slots, width), bf16),
            pltpu.VMEM(block, f32),
            pltpu.VMEM(block, f32),
            pltpu.VMEM(block, f32),
            pltpu.VMEM(block, f32),
            pltpu.VMEM((classes, 8, TILE), f32),
            pltpu.VMEM((NZ, NY, 8, TILE), f32),
            pltpu.VMEM((NZ, NY, img_rows, col), bf16),
            pltpu.VMEM((NZ, owners, 2 * TILE), f32),
            pltpu.VMEM((8, owners, TILE), f32),
            pltpu.VMEM((NZ, owners, 2 * TILE), f32),
            dma((6,)),
            dma((classes,)),
            dma((classes,)),
            dma((messages,)),
            dma((messages,)),
            dma((messages,)),
            dma((messages,)),
            dma((NX,)),
            dma((NX,)),
            dma((NX,)),
            dma((NX,)),
            dma((classes,)),
            dma((classes,)),
            dma((NY + NZ,)),
            dma((NY + NZ,)),
            dma((3, NZ)),
            dma((NZ,)),
        ],
        compiler_params=pltpu.CompilerParams(
            collective_id=0, has_side_effects=True, vmem_limit_bytes=28 * 1024 * 1024
        ),
        name="estep",
    )(images, projection, prior, listed, shells, noise)


def sums_kernel(shared, packed, out_ref, stage, out_sem):
    owners = packed.shape[0]
    orients = shared.shape[2]

    def out_copy(o, s):
        return pltpu.make_async_copy(
            stage.at[s], out_ref.at[pl.ds(pl.multiple_of(o * orients, 16), orients), :], out_sem.at[s]
        )

    depth = stage.shape[0] // 2

    def emit(t, carry):
        base = lax.rem(t, 2) * depth

        @pl.when(t > 1)
        def _():
            for s in range(depth):
                out_copy((t - 2) * depth + s, base + s).wait()

        for s in range(depth):
            o = t * depth + s
            stage[base + s] = jnp.dot(
                shared[o // NY, o % NY], packed[o], preferred_element_type=jnp.float32
            ).astype(jnp.bfloat16)
        for s in range(depth):
            out_copy(t * depth + s, base + s).start()
        return carry

    rounds = owners // depth
    lax.fori_loop(0, rounds, emit, 0)
    for t in (rounds - 2, rounds - 1):
        for s in range(depth):
            out_copy(t * depth + s, (t % 2) * depth + s).wait()


def sums(shared, packed):
    owners, slots, col = packed.shape
    orients = shared.shape[2]
    vmem = pl.BlockSpec(memory_space=pltpu.VMEM)
    return pl.pallas_call(
        sums_kernel,
        out_shape=jax.ShapeDtypeStruct((owners * orients, col), jnp.bfloat16),
        in_specs=[vmem, vmem],
        out_specs=pl.BlockSpec(memory_space=pltpu.HBM),
        scratch_shapes=[pltpu.VMEM((8, orients, col), jnp.bfloat16), pltpu.SemaphoreType.DMA((8,))],
        compiler_params=pltpu.CompilerParams(vmem_limit_bytes=8 * 1024 * 1024),
        name="sums",
    )(shared, packed)


def body(images, projections, log_prior, significant, shell_index, noise_inv):
    owners = lax.axis_size("ori")
    rows, width = images.shape
    listed = significant.shape[1]
    cap = max(2, 3 * rows * listed // (2 * owners))
    shared, packed, evidence = step(
        pltpu.with_memory_space_constraint(images, pltpu.HBM),
        pltpu.with_memory_space_constraint(projections[0], pltpu.HBM),
        pltpu.with_memory_space_constraint(log_prior, pltpu.HBM),
        pltpu.with_memory_space_constraint(significant.T, pltpu.HBM),
        pltpu.with_memory_space_constraint(shell_index.reshape(width // TILE, TILE), pltpu.HBM),
        pltpu.with_memory_space_constraint(noise_inv, pltpu.HBM),
        owners * cap,
        width // owners,
    )
    return (sums(shared, packed)[None], evidence[0])


def solution(mesh):
    in_specs = (P("ori", None), P("cls", "ori", None), P("cls", "ori"), P("ori", None), P(), P())
    out_specs = (P("cls", None, "ori"), P("ori"))
    return jax.shard_map(body, mesh=mesh, in_specs=in_specs, out_specs=out_specs, check_vma=False)
```

```python
import jax
import jax.numpy as jnp
from jax import lax
from jax.experimental import pallas as pl
from jax.experimental.pallas import tpu as pltpu
from jax.sharding import PartitionSpec as P

MESH = pl.DeviceIdType.MESH
SENTINEL = -1e30
TILE = 128
NY = 4
NZ = 8
NX = 4


def mod(value, size):
    return lax.rem(value + size, size)


class Ring:
    def __init__(self, buf, view, pos, sizes, devs, send_sem, recv_sem):
        self.buf, self.view, self.pos, self.sizes, self.devs = buf, view, pos, sizes, devs
        self.send_sem, self.recv_sem = send_sem, recv_sem
        self.started = []
        nf = sizes[0]
        offsets = [0]
        for r in range(1, nf // 2):
            offsets += [-r, r]
        offsets.append(nf // 2)
        self.offsets = offsets

    def copy(self, ident, df, dg, n, r, d, ring):
        (f, g), (nf, ng) = self.pos, self.sizes
        half = d if r == n // 2 - 1 else None
        ref = self.view(self.buf, mod(f + df, nf), mod(g + dg, ng), half)
        return pltpu.make_async_remote_copy(
            src_ref=ref,
            dst_ref=ref,
            send_sem=self.send_sem.at[ident],
            recv_sem=self.recv_sem.at[ident],
            device_id=self.devs[ring](1 - 2 * d),
            device_id_type=MESH,
        )

    def send(self, *what):
        self.copy(*what).start()
        self.started.append(what)

    def f_what(self, r, d, hop):
        return (2 * r + d, -(1 - 2 * d) * (r + hop), 0, self.sizes[0], r, d, 0)

    def g_what(self, j, r, d, hop):
        nf, ng = self.sizes
        return (nf + (j * (ng // 2) + r) * 2 + d, self.offsets[j], -(1 - 2 * d) * (r + hop), ng, r, d, 1)

    def start(self):
        for d in (0, 1):
            self.send(*self.f_what(0, d, 0))
            self.send(*self.g_what(0, 0, d, 0))

    def f_rounds(self):
        return self.sizes[0] // 2

    def f_round(self, r):
        nf = self.sizes[0]
        for d in (0, 1):
            self.copy(*self.f_what(r, d, 1)).wait_recv()
            if r + 1 < nf // 2:
                self.send(*self.f_what(r + 1, d, 0))
        for j in (2 * r + 1, 2 * r + 2):
            if j < nf:
                for d in (0, 1):
                    self.send(*self.g_what(j, 0, d, 0))

    def g_step(self, i):
        nf, ng = self.sizes
        r, j = i // nf, i % nf
        for d in (0, 1):
            self.copy(*self.g_what(j, r, d, 1)).wait_recv()
            if r + 1 < ng // 2:
                self.send(*self.g_what(j, r + 1, d, 0))

    def finish(self):
        for what in self.started:
            self.copy(*what).wait_send()


def lines_of(top, full):
    row = lax.broadcasted_iota(jnp.int32, (8, TILE), 0)
    out = jnp.zeros((8, TILE), jnp.float32)
    at = 0
    for value in (top, full):
        for t in range(value.shape[1] // TILE):
            out = jnp.where(row == at, value[:, t * TILE : (t + 1) * TILE], out)
            at += 1
    return out


def step_kernel(
    img_ref,
    proj_ref,
    prior_in,
    listed_in,
    shell_in,
    noise_ref,
    shared,
    packed,
    evidence_ref,
    prior_ref,
    listed_ref,
    shell_ref,
    evidence,
    weights,
    images,
    proj,
    norms,
    received,
    part,
    from_pair,
    summed,
    from_far,
    stat,
    spread,
    band,
    ranks,
    tops,
    share,
    own_sem,
    proj_send,
    proj_recv,
    img_send,
    img_recv,
    post_send,
    post_recv,
    pair_send,
    pair_recv,
    far_send,
    far_recv,
    stat_send,
    stat_recv,
    spread_send,
    spread_recv,
    band_send,
    band_recv,
):
    cls = lax.axis_index("cls")
    ori = lax.axis_index("ori")
    x, core = cls // 2, cls % 2
    z, y = ori // NY, ori % NY
    classes = 2 * NX
    owners = NY * NZ
    img_rows = images.shape[2]
    width = proj.shape[2]
    col = band.shape[3]
    slots = received.shape[0]
    orients = proj.shape[1]
    cap = slots // owners
    tiles = slots // TILE

    def slot_of(k):
        return (k % 2) * NX + k // 2

    def peer(d, sign):
        c = (core + d) % 2
        return mod(x + sign * (d // 2), NX) * 2 + c

    def cls_dev(k):
        return (k, ori)

    def y_dev(step):
        return (cls, z * NY + mod(y + step, NY))

    def z_dev(step):
        return (cls, mod(z + step, NZ) * NY + y)

    small = [
        pltpu.make_async_copy(src, dst, own_sem.at[3 + i])
        for i, (src, dst) in enumerate(((shell_in, shell_ref), (listed_in, listed_ref), (prior_in, prior_ref)))
    ]
    for cp in small:
        cp.start()
    barrier = pltpu.get_barrier_semaphore()
    greeted = [cls_dev(peer(d, 1)) for d in range(1, classes)]
    greeted += [y_dev(d) for d in range(1, NY)]
    greeted += [z_dev(d) for d in range(1, NZ)]
    for dev in greeted:
        pl.semaphore_signal(barrier, inc=1, device_id=dev, device_id_type=MESH)
    own_img = pltpu.make_async_copy(
        img_ref.at[:, pl.ds(pl.multiple_of(cls * width, TILE), width)], received.at[0:img_rows], own_sem.at[0]
    )
    own_img.start()
    own_proj = pltpu.make_async_copy(
        proj_ref.at[:, pl.ds(pl.multiple_of(cls * width, TILE), width)], proj.at[slot_of(cls)], own_sem.at[1]
    )
    own_proj.start()
    for cp in small:
        cp.wait()
    shells = shell_ref[...]
    level = jnp.zeros(shells.shape, jnp.float32)
    for j in range(noise_ref.shape[0]):
        level = jnp.where(shells == j, noise_ref[j], level)
    weights[...] = level
    named = jnp.zeros((owners, img_rows), jnp.bool_)
    block_row = lax.broadcasted_iota(jnp.int32, (owners, img_rows), 0)
    for j in range(listed_ref.shape[0]):
        named = jnp.logical_or(named, listed_ref[j : j + 1, :] == block_row)
    named = jnp.where(named, 1.0, 0.0).astype(jnp.bfloat16)
    image_row = lax.broadcasted_iota(jnp.int32, (img_rows, TILE), 0)
    image_lane = lax.broadcasted_iota(jnp.int32, (img_rows, TILE), 1) % img_rows
    twice = jnp.where(image_row == image_lane, 1.0, 0.0).astype(jnp.bfloat16)
    before = jnp.where(image_row < image_lane, 1.0, 0.0).astype(jnp.bfloat16)
    there = jnp.dot(named, twice, preferred_element_type=jnp.float32)
    rank = jnp.dot(named, before, preferred_element_type=jnp.float32)
    rank = jnp.where(there > 0.5, rank, -1.0)
    rank = jnp.concatenate([rank, jnp.zeros((img_rows - owners, TILE), jnp.float32)], axis=0)
    images[z, y, :, width : width + TILE] = rank.astype(jnp.bfloat16)

    def weight_row(j):
        return weights[pl.ds(cls * (width // TILE) + j, 1), :]

    pl.semaphore_wait(barrier, len(greeted))

    def proj_copy(d, to, frm):
        return pltpu.make_async_remote_copy(
            src_ref=proj_ref.at[:, pl.ds(pl.multiple_of(to * width, TILE), width)],
            dst_ref=proj.at[slot_of(frm)],
            send_sem=proj_send.at[d],
            recv_sem=proj_recv.at[d],
            device_id=cls_dev(to),
            device_id_type=MESH,
        )

    for d in (2, 3, 6, 7, 4, 5, 1):
        proj_copy(d, peer(d, 1), cls).start()
    own_img.wait()
    for j in range(width // TILE):
        lane = slice(j * TILE, (j + 1) * TILE)
        images[z, y, :, lane] = (received[0:img_rows, lane].astype(jnp.float32) * weight_row(j)).astype(jnp.bfloat16)

    def slice_view(swap):
        def view(buf, fi, gi, half):
            zi, yi = (fi, gi) if swap else (gi, fi)
            n = buf.shape[2]
            if half is None:
                return buf.at[zi, yi]
            return buf.at[zi, yi, pl.ds(half * (n // 2), n // 2)]

        return view

    def gather(buf, send_sem, recv_sem, f_hooks, g_hooks):
        rings = (
            Ring(buf, slice_view(False), (y, z), (NY, NZ), (y_dev, z_dev), send_sem, recv_sem),
            Ring(buf, slice_view(True), (z, y), (NZ, NY), (z_dev, y_dev), send_sem, recv_sem),
        )

        def both(act):
            for c in range(2):

                @pl.when(core == c)
                def _():
                    act(rings[c])

        both(lambda ring: ring.start())
        for r in range(NZ // 2):
            both(lambda ring: ring.f_round(r) if r < ring.f_rounds() else None)
            for hook in f_hooks.get(r, ()):
                hook()
        for i in range(NY * NZ // 2):
            both(lambda ring: ring.g_step(i))
            for hook in g_hooks.get(i, ()):
                hook()
        both(lambda ring: ring.finish())

    def norm_of(d):
        def run():
            if d == 0:
                own_proj.wait()
            else:
                proj_copy(d, peer(d, 1), peer(d, -1)).wait_recv()
            at = slot_of(peer(d, -1)) if d else slot_of(cls)
            norm = jnp.zeros((orients, TILE), jnp.float32)
            for j in range(width // TILE):
                lane = slice(j * TILE, (j + 1) * TILE)
                wide = proj[at, :, lane].astype(jnp.float32)
                norm = norm + wide * wide * weight_row(j)
            norms[at] = 0.5 * jnp.sum(norm, axis=1, keepdims=True)

        return run

    order = (0, 1, 2, 3, 6, 7)
    gather(images, img_send, img_recv, {}, {10 + i: [norm_of(d)] for i, d in enumerate(order)})

    owner_x, owner_core = z // 2, z % 2
    role = mod(x - owner_x, NX)
    on_line = core == owner_core
    half = NZ // 2
    band_cols = pl.ds(pl.multiple_of(y * col, TILE), col)
    ahead = (mod(x + 1, NX) * 2 + core, ori)
    behind = (mod(x - 1, NX) * 2 + core, ori)
    pair = (x * 2 + 1 - core, ori)
    is_owner = jnp.logical_and(on_line, role == 0)

    def band_copy(j, lane, first):
        return pltpu.make_async_remote_copy(
            src_ref=images.at[j, :, :, band_cols] if first else band.at[j],
            dst_ref=band.at[j],
            send_sem=band_send.at[lane, j],
            recv_sem=band_recv.at[j],
            device_id=(ahead, behind, pair)[lane],
            device_id_type=MESH,
        )

    own_band = pltpu.make_async_copy(images.at[:, :, :, band_cols], band, own_sem.at[2])

    def band_first(js):
        @pl.when(is_owner)
        def _():
            for j in js:
                band_copy(j, 0, True).start()
                band_copy(half + j, 1, True).start()
            for j in js:
                band_copy(j, 2, True).start()
                band_copy(half + j, 2, True).start()

    def relay_plan(s):
        near, mid, far = s - 1, s - 2, s - 3
        plan = {1: [], 2: [], 3: []}
        if 0 <= near < half:
            plan[1].append((near, 0))
            plan[3].append((half + near, 1))
        if 0 <= mid < half:
            plan[2] += [(mid, 0), (half + mid, 1)]
        if 0 <= far < half:
            plan[1].append((half + far, None))
            plan[3].append((far, None))
        return plan

    def band_step(s):
        def run():
            for k, todo in relay_plan(s).items():

                @pl.when(jnp.logical_and(on_line, role == k))
                def _():
                    for j, lane in todo:
                        band_copy(j, 2, False).wait_recv()
                        if lane is not None:
                            band_copy(j, lane, False).start()
                        band_copy(j, 2, False).start()

        return run

    def nth_piece(n):
        return jnp.where(
            role == 3, (n + half) % NZ, jnp.where(role == 2, (n % 2) * half + n // 2, n)
        )

    def band_sent():
        @pl.when(is_owner)
        def _():
            for j in range(half):
                band_copy(j, 0, True).wait_send()
                band_copy(half + j, 1, True).wait_send()
            for j in range(NZ):
                band_copy(j, 2, True).wait_send()

        for k in (1, 2, 3):

            @pl.when(jnp.logical_and(on_line, role == k))
            def _():
                for s in range(1, half + 3):
                    for j, lane in relay_plan(s)[k]:
                        if lane is not None:
                            band_copy(j, lane, False).wait_send()
                        band_copy(j, 2, False).wait_send()

    @pl.when(is_owner)
    def _():
        own_band.start()

    band_first((0, 1))

    lanes = NY * img_rows
    lane_src = lax.broadcasted_iota(jnp.int32, (NY * cap, lanes), 1) // img_rows
    row_id = lax.broadcasted_iota(jnp.int32, (NY * cap, lanes), 0)
    place = jnp.where(lane_src == row_id // cap, (row_id % cap).astype(jnp.float32), -2.0)
    o_row = lax.broadcasted_iota(jnp.int32, (owners, TILE), 0) == ori
    low = lax.broadcasted_iota(jnp.int32, (owners, TILE), 1) < img_rows

    def pick_rows(zi, carry):
        tables = [
            images[zi, yi, 0:owners, width : width + TILE].astype(jnp.float32) for yi in range(NY)
        ]
        both = [jnp.where(low, tables[0], tables[1]), jnp.where(low, tables[2], tables[3])]
        for h in range(2):
            ranks[zi, :, h * TILE : (h + 1) * TILE] = both[h]
        line = jnp.concatenate(
            [jnp.sum(jnp.where(o_row, both[h], 0.0), axis=0, keepdims=True) for h in range(2)], axis=1
        )
        pick = jnp.where(place == line, 1.0, 0.0).astype(jnp.bfloat16)
        data = images[zi, :, :, 0:width].reshape(lanes, width)
        found = jnp.dot(pick, data, preferred_element_type=jnp.float32)
        received[pl.ds(pl.multiple_of(zi * NY * cap, 16), NY * cap), :] = found.astype(jnp.bfloat16)
        return carry

    lax.fori_loop(0, NZ, pick_rows, 0)
    for d in range(1, classes):
        if d not in order:
            norm_of(d)()

    def pair_copy(j):
        return pltpu.make_async_remote_copy(
            src_ref=part.at[j],
            dst_ref=from_pair.at[j],
            send_sem=pair_send.at[j],
            recv_sem=pair_recv.at[j],
            device_id=pair,
            device_id_type=MESH,
        )

    def far_copy(dx):
        return pltpu.make_async_remote_copy(
            src_ref=summed.at[mod(x + dx, NX)],
            dst_ref=from_far.at[dx],
            send_sem=far_send.at[dx],
            recv_sem=far_recv.at[dx],
            device_id=(mod(x + dx, NX) * 2 + core, ori),
            device_id_type=MESH,
        )

    def partial(c):
        block = proj[pl.ds(c * NX, NX)].reshape(NX * orients, width)
        score = lax.dot_general(block, received[...], (((1,), (1,)), ((), ())), preferred_element_type=jnp.float32)
        return score.reshape(NX, orients, slots) - norms[pl.ds(c * NX, NX)]

    part[...] = partial(1 - core)
    for j in range(NX):
        pair_copy(j).start()
    summed[...] = partial(core)
    for dx in (2, 1, 3):
        j = mod(x + dx, NX)
        pair_copy(j).wait_recv()
        summed[j] = summed[j] + from_pair[j]
        far_copy(dx).start()
    band_step(1)()
    band_first((2, 3))
    pair_copy(x).wait_recv()
    square = (orients, orients)
    diagonal = lax.broadcasted_iota(jnp.int32, square, 0) == lax.broadcasted_iota(jnp.int32, square, 1)
    prior = jnp.sum(jnp.where(diagonal, jnp.broadcast_to(prior_ref[...], square), 0.0), axis=1, keepdims=True)
    total = summed[x] + from_pair[x] + prior
    for dx in range(1, NX):
        far_copy(dx).wait_recv()
        total = total + from_far[dx]
    score = total
    peak = jnp.max(score, axis=0, keepdims=True)
    amount = jnp.sum(jnp.exp(score - peak), axis=0, keepdims=True)
    stat[cls] = lines_of(peak, amount)

    def stat_copy(d, frm):
        return pltpu.make_async_remote_copy(
            src_ref=stat.at[frm],
            dst_ref=stat.at[frm],
            send_sem=stat_send.at[d],
            recv_sem=stat_recv.at[d],
            device_id=cls_dev(peer(d, 1)),
            device_id_type=MESH,
        )

    for d in range(1, classes):
        stat_copy(d, cls).start()
    for d in range(1, classes):
        stat_copy(d, peer(d, -1)).wait_recv()
    top = []
    full = []
    for t in range(tiles):
        best = stat[0, t : t + 1]
        for k in range(1, classes):
            best = jnp.maximum(best, stat[k, t : t + 1])
        whole = jnp.zeros_like(best)
        for k in range(classes):
            whole = whole + stat[k, tiles + t : tiles + t + 1] * jnp.exp(stat[k, t : t + 1] - best)
        top.append(best)
        full.append(whole)
    top = jnp.concatenate(top, axis=1)
    full = jnp.concatenate(full, axis=1)
    spread[z, y] = lines_of(top, full)

    def spread_y(d, yi):
        return pltpu.make_async_remote_copy(
            src_ref=spread.at[z, yi],
            dst_ref=spread.at[z, yi],
            send_sem=spread_send.at[d],
            recv_sem=spread_recv.at[d],
            device_id=y_dev(d),
            device_id_type=MESH,
        )

    def spread_z(d, zi):
        return pltpu.make_async_remote_copy(
            src_ref=spread.at[zi],
            dst_ref=spread.at[zi],
            send_sem=spread_send.at[NY + d],
            recv_sem=spread_recv.at[NY + d],
            device_id=z_dev(d),
            device_id_type=MESH,
        )

    for d in range(1, NY):
        spread_y(d, y).start()
    shared[z, y] = jnp.exp(score - top).astype(jnp.bfloat16)

    def spread_on():
        for d in range(1, NY):
            spread_y(d, mod(y - d, NY)).wait_recv()
        for d in range(1, NZ):
            spread_z(d, z).start()

    def spread_end():
        for d in range(1, NZ):
            spread_z(d, mod(z - d, NZ)).wait_recv()
        for zi in range(NZ):
            for yi in range(NY):
                o = zi * NY + yi
                for t in range(2 * tiles):
                    tops[t, o : o + 1, :] = spread[zi, yi, t : t + 1, :]

    def shares_of(qs):
        def run():
            lanes_of = {q: slice((q % 2) * TILE, (q % 2 + 1) * TILE) for q in qs}
            rank = {q: ranks[q // 2, :, lanes_of[q]].astype(jnp.int32) for q in qs}
            named = {q: rank[q] >= 0 for q in qs}
            spot = {
                q: jnp.maximum(rank[q], 0) + jnp.where(low, 2 * q * cap, (2 * q + 1) * cap) for q in qs
            }

            def look(q, base):
                first, last = 2 * q * cap // TILE, (2 * (q + 1) * cap - 1) // TILE
                found = None
                for t in range(first, last + 1):
                    local = spot[q] - t * TILE
                    value = jnp.take_along_axis(tops[base + t], jnp.clip(local, 0, TILE - 1), axis=1)
                    found = value if found is None else jnp.where(local >= 0, value, found)
                return found

            highs = {q: jnp.where(named[q], look(q, 0), SENTINEL) for q in qs}
            wholes = {q: jnp.where(named[q], look(q, tiles), 0.0) for q in qs}
            best = {q: jnp.max(highs[q], axis=0, keepdims=True) for q in qs}
            raised = {q: jnp.where(named[q], jnp.exp(highs[q] - best[q]), 0.0) for q in qs}
            whole = {q: jnp.sum(raised[q] * wholes[q], axis=0, keepdims=True) for q in qs}
            part_of = {q: raised[q] / whole[q] for q in qs}
            for q in qs:
                share[q // 2, :, lanes_of[q]] = part_of[q]
                evidence[q : q + 1, :] = best[q] + jnp.log(whole[q])

        return run

    def pack(n):
        def run():
            g = nth_piece(n)

            @pl.when(jnp.logical_not(on_line))
            def _():
                band_copy(g, 2, False).wait_recv()

            data = band[g].reshape(lanes, col)
            blocks = 8

            def some(b, carry):
                first = pl.multiple_of(b * blocks, blocks)
                table = ranks[g, pl.ds(first, blocks), :]
                factor = share[g, pl.ds(first, blocks), :]
                picks = [
                    jnp.where(place == table[i : i + 1], factor[i : i + 1], 0.0).astype(jnp.bfloat16)
                    for i in range(blocks)
                ]
                found = jnp.dot(
                    jnp.concatenate(picks, axis=0), data, preferred_element_type=jnp.float32
                ).astype(jnp.bfloat16)
                packed[pl.ds(first, blocks), pl.ds(pl.multiple_of(g * NY * cap, 16), NY * cap), :] = found.reshape(
                    blocks, NY * cap, col
                )
                return carry

            lax.fori_loop(0, owners // blocks, some, 0)

        return run

    def quarter(n):
        return shares_of(range(n * 4, n * 4 + 4))

    hooks = {
        0: [spread_end],
        1: [quarter(0)],
        2: [quarter(1)],
        3: [band_step(3), quarter(2)],
        4: [quarter(3)],
        5: [pack(0)],
        6: [band_step(4), pack(1)],
        7: [pack(2)],
        8: [pack(3)],
        9: [band_step(5), pack(4)],
        10: [pack(5)],
        11: [pack(6)],
        12: [band_step(6)],
        13: [pack(7)],
    }

    @pl.when(is_owner)
    def _():
        own_band.wait()

    gather(shared, post_send, post_recv, {0: [spread_on], 1: [band_step(2)]}, hooks)

    line = evidence[pl.ds(ori // 2, 1), :]
    other = pltpu.roll(line, img_rows, 1)
    evidence_ref[...] = jnp.where(ori % 2 == 0, line, other)[:, 0:img_rows]
    band_sent()
    for d in range(1, classes):
        proj_copy(d, peer(d, 1), cls).wait_send()
        stat_copy(d, cls).wait_send()
    for j in range(NX):
        pair_copy(j).wait_send()
        if j:
            far_copy(j).wait_send()
    for d in range(1, NY):
        spread_y(d, y).wait_send()
    for d in range(1, NZ):
        spread_z(d, z).wait_send()


def step(images, projection, prior, listed, shells, noise, slots, col):
    img_rows, freqs = images.shape
    orients = projection.shape[0]
    width = freqs // (2 * NX)
    wide = width + TILE
    owners = NY * NZ
    dma = pltpu.SemaphoreType.DMA
    classes = 2 * NX
    messages = NZ + NZ * NY
    block = (NX, orients, slots)
    vmem = pl.BlockSpec(memory_space=pltpu.VMEM)
    bf16, f32 = jnp.bfloat16, jnp.float32
    return pl.pallas_call(
        step_kernel,
        out_shape=(
            jax.ShapeDtypeStruct((NZ, NY, orients, slots), bf16),
            jax.ShapeDtypeStruct((owners, slots, col), bf16),
            jax.ShapeDtypeStruct((1, img_rows), f32),
        ),
        in_specs=[
            pl.BlockSpec(memory_space=pltpu.HBM),
            pl.BlockSpec(memory_space=pltpu.HBM),
            pl.BlockSpec(memory_space=pltpu.HBM),
            pl.BlockSpec(memory_space=pltpu.HBM),
            pl.BlockSpec(memory_space=pltpu.HBM),
            pl.BlockSpec(memory_space=pltpu.SMEM),
        ],
        out_specs=(vmem, vmem, vmem),
        scratch_shapes=[
            pltpu.VMEM(prior.shape, f32),
            pltpu.VMEM(listed.shape, jnp.int32),
            pltpu.VMEM(shells.shape, jnp.int32),
            pltpu.VMEM((owners // 2, TILE), f32),
            pltpu.VMEM(shells.shape, f32),
            pltpu.VMEM((NZ, NY, img_rows, wide), bf16),
            pltpu.VMEM((classes, orients, width), bf16),
            pltpu.VMEM((classes, orients, 1), f32),
            pltpu.VMEM((slots, width), bf16),
            pltpu.VMEM(block, f32),
            pltpu.VMEM(block, f32),
            pltpu.VMEM(block, f32),
            pltpu.VMEM(block, f32),
            pltpu.VMEM((classes, 8, TILE), f32),
            pltpu.VMEM((NZ, NY, 8, TILE), f32),
            pltpu.VMEM((NZ, NY, img_rows, col), bf16),
            pltpu.VMEM((NZ, owners, 2 * TILE), f32),
            pltpu.VMEM((8, owners, TILE), f32),
            pltpu.VMEM((NZ, owners, 2 * TILE), f32),
            dma((6,)),
            dma((classes,)),
            dma((classes,)),
            dma((messages,)),
            dma((messages,)),
            dma((messages,)),
            dma((messages,)),
            dma((NX,)),
            dma((NX,)),
            dma((NX,)),
            dma((NX,)),
            dma((classes,)),
            dma((classes,)),
            dma((NY + NZ,)),
            dma((NY + NZ,)),
            dma((3, NZ)),
            dma((NZ,)),
        ],
        compiler_params=pltpu.CompilerParams(
            collective_id=0, has_side_effects=True, vmem_limit_bytes=28 * 1024 * 1024
        ),
        name="estep",
    )(images, projection, prior, listed, shells, noise)


def sums_kernel(shared, packed, out_ref, stage, out_sem):
    owners = packed.shape[0]
    orients = shared.shape[2]

    def out_copy(o, s):
        return pltpu.make_async_copy(
            stage.at[s], out_ref.at[pl.ds(pl.multiple_of(o * orients, 16), orients), :], out_sem.at[s]
        )

    depth = stage.shape[0] // 2

    def emit(t, carry):
        base = lax.rem(t, 2) * depth

        @pl.when(t > 1)
        def _():
            for s in range(depth):
                out_copy((t - 2) * depth + s, base + s).wait()

        for s in range(depth):
            o = t * depth + s
            stage[base + s] = jnp.dot(
                shared[o // NY, o % NY], packed[o], preferred_element_type=jnp.float32
            ).astype(jnp.bfloat16)
        for s in range(depth):
            out_copy(t * depth + s, base + s).start()
        return carry

    rounds = owners // depth
    lax.fori_loop(0, rounds, emit, 0)
    for t in (rounds - 2, rounds - 1):
        for s in range(depth):
            out_copy(t * depth + s, (t % 2) * depth + s).wait()


def sums(shared, packed):
    owners, slots, col = packed.shape
    orients = shared.shape[2]
    vmem = pl.BlockSpec(memory_space=pltpu.VMEM)
    return pl.pallas_call(
        sums_kernel,
        out_shape=jax.ShapeDtypeStruct((owners * orients, col), jnp.bfloat16),
        in_specs=[vmem, vmem],
        out_specs=pl.BlockSpec(memory_space=pltpu.HBM),
        scratch_shapes=[pltpu.VMEM((8, orients, col), jnp.bfloat16), pltpu.SemaphoreType.DMA((8,))],
        compiler_params=pltpu.CompilerParams(vmem_limit_bytes=8 * 1024 * 1024),
        name="sums",
    )(shared, packed)


def body(images, projections, log_prior, significant, shell_index, noise_inv):
    owners = lax.axis_size("ori")
    rows, width = images.shape
    listed = significant.shape[1]
    cap = max(2, 3 * rows * listed // (2 * owners))
    shared, packed, evidence = step(
        pltpu.with_memory_space_constraint(images, pltpu.HBM),
        pltpu.with_memory_space_constraint(projections[0], pltpu.HBM),
        pltpu.with_memory_space_constraint(log_prior, pltpu.HBM),
        pltpu.with_memory_space_constraint(significant.T, pltpu.HBM),
        pltpu.with_memory_space_constraint(shell_index.reshape(width // TILE, TILE), pltpu.HBM),
        pltpu.with_memory_space_constraint(noise_inv, pltpu.HBM),
        owners * cap,
        width // owners,
    )
    return (sums(shared, packed)[None], evidence[0])


def solution(mesh):
    in_specs = (P("ori", None), P("cls", "ori", None), P("cls", "ori"), P("ori", None), P(), P())
    out_specs = (P("cls", None, "ori"), P("ori"))
    return jax.shard_map(body, mesh=mesh, in_specs=in_specs, out_specs=out_specs, check_vma=False)
```
